32 devices in a mesh: loop: 16 (over z, y, core), narrow: 2 (over x).
Axes of the slice: x: 2, y: 2, z: 4, core: 2. Of those that a mesh axis runs over, the one named last changes fastest.
Arguments:
- queries: bfloat16 [8192, 4096], P(('loop', 'narrow')), may hold values from -2 to 2
- passages: bfloat16 [64, 4096], P('loop'), may hold values from -10 to 10
- pos_ids: int32 [8192], P(('loop', 'narrow')), may hold values from 0 to 63
- neg_ids: int32 [8192, 32], P(('loop', 'narrow')), may hold values from 0 to 63
- neg_mask: int32 [8192, 32], P(('loop', 'narrow')), may hold values 0 or 1
- neg_counts: int32 [8192], P(('loop', 'narrow')), may hold values from 0 to 32
- d_loss: float32 [8192], P(('loop', 'narrow')), may hold values from -6 to 6
Outputs:
- query_loss: float32 [8192], P(('loop', 'narrow'))
- grad_queries: bfloat16 [8192, 4096], P(('loop', 'narrow'))
- grad_passages: bfloat16 [64, 4096], P('loop')
The draws below stay inside these ranges and needn't reach their ends.
Inputs may be any that keep to these rules, and one draw needn't show every extreme that they name: `neg_counts`: slots at or beyond a query's count are padding.
All inputs are finite; a program needn't handle non-finite values. No bound on the sum of `neg_mask` on one device may be relied on, other than what follows from the above.
Results may differ from the reference program's by a relative error of at most 0.0058.
Values may be sent and summed in bfloat16 or wider, within the bound.
No kernel may reach another device: no remote copies, remote signals or barrier semaphores. Data moves between devices by JAX's collectives and lax.ppermute only.
A program may use at most 64 MiB of HBM per device.

```python
import math
import jax
import jax.numpy as jnp
from jax import lax

D = 4096
NEG = 32
QDEV = 256
NQ = 8192
NP = 64


def scaled_rows(key, count, base):
    key_vals, key_rows = jax.random.split(key, 2)
    rows = jnp.exp(jax.random.uniform(key_rows, (count, 1), jnp.float32, 0.0, math.log(10.0)))
    values = jnp.clip(jax.random.normal(key_vals, (count, D), jnp.float32), -4.0, 4.0)
    return values * rows * base


def draw_queries(key, part):
    return scaled_rows(jax.random.fold_in(key, 11), NQ, 0.01).astype(jnp.bfloat16)


def draw_passages(key, part):
    return scaled_rows(jax.random.fold_in(key, 23), NP, 0.05).astype(jnp.bfloat16)


def place_ends(values, rng, smallest, largest):
    place = [jax.random.randint(jax.random.fold_in(rng, axis), (), 0, length) for axis, length in enumerate(values.shape)]
    widest = values.shape.index(max(values.shape))
    beside = place[:widest] + [(place[widest] + 1) % values.shape[widest]] + place[widest + 1:]
    return values.at[tuple(place)].set(smallest).at[tuple(beside)].set(largest)


def block_levels(rng, extent, shards, low, largest):
    factor_of, own = 1.0, jax.random.fold_in(rng, 6)
    for axis_at, shards_of in shards:
        steps = jnp.exp(jax.random.uniform(jax.random.fold_in(own, axis_at), (shards_of,), jnp.float32, low / len(shards), largest / len(shards)))
        factor_of = factor_of * jnp.repeat(steps, extent[axis_at] // shards_of).reshape([-1 if axis == axis_at else 1 for axis in range(len(extent))])
    return factor_of


def bell_draw(own_key, shape, spread, most, cuts=(), held_as=jnp.bfloat16):
    loudness = block_levels(own_key, shape, cuts, -0.22, 0.18) if cuts else 1.0
    result = jax.random.normal(own_key, shape, jnp.float32) * spread * loudness
    return jnp.minimum(jnp.maximum(result, -most), most).astype(held_as)


def setup_inputs(seed: int = 0) -> dict:
    seeds = jax.random.split(jax.random.key(seed), 8)
    queries = draw_queries(jax.random.fold_in(seeds[7], 71), 0)
    passages = draw_passages(jax.random.fold_in(seeds[7], 71), 0)
    pos_ids = place_ends(jax.random.randint(seeds[2], (NQ,), 0, NP), jax.random.fold_in(seeds[2], 1), 0, NP - 1).astype(jnp.int32)
    neg_ids = place_ends(jax.random.randint(seeds[3], (NQ, NEG), 0, NP), jax.random.fold_in(seeds[3], 1), 0, NP - 1).astype(jnp.int32)
    neg_mask = place_ends((jax.random.randint(seeds[4], (NQ, NEG), 0, 4) < 3).astype(jnp.int32), jax.random.fold_in(seeds[4], 1), 0, 1)
    neg_counts = place_ends(jax.random.randint(seeds[5], (NQ,), 0, NEG + 1), jax.random.fold_in(seeds[5], 1), 0, NEG).astype(jnp.int32)
    d_loss = bell_draw(seeds[6], (NQ,), 1.0, 6.0, ((0, 32),), jnp.float32)
    return dict(queries=queries, passages=passages, pos_ids=pos_ids, neg_ids=neg_ids, neg_mask=neg_mask, neg_counts=neg_counts, d_loss=d_loss)


logit_scale = 50.0
norm_eps = 1e-06

def normalize(rows):
    wide = rows.astype(jnp.float32)
    scales = lax.rsqrt(lax.optimization_barrier(jnp.sum(wide * wide, axis=-1)) + norm_eps)
    return (scales, (wide * scales[:, None]).astype(jnp.bfloat16))

def weight_table(valid, neg_ids, pool_size):
    columns = jnp.arange(pool_size, dtype=jnp.int32)
    weights = jnp.ones((neg_ids.shape[0], pool_size), jnp.float32)
    for first in range(0, NEG, 8):
        named = neg_ids[:, first:first + 8]
        usable = valid[:, first:first + 8]
        hits = (named[:, :, None] == columns[None, None, :]) & usable[:, :, None]
        weights = weights + lax.optimization_barrier(jnp.sum(hits.astype(jnp.float32), axis=1))
    return weights

def tangent_back(rows, scales, direction):
    unit = rows.astype(jnp.float32) * scales[:, None]
    inner = lax.optimization_barrier(jnp.sum(unit * direction, axis=-1, keepdims=True))
    return (scales[:, None] * (direction - unit * inner)).astype(jnp.bfloat16)

def reference(queries, passages, pos_ids, neg_ids, neg_mask, neg_counts, d_loss):
    pool_size = passages.shape[0]
    pscale, pnorm = normalize(passages)
    columns = jnp.arange(pool_size, dtype=jnp.int32)
    slots = jnp.arange(NEG, dtype=jnp.int32)
    groups = queries.shape[0] // QDEV

    def one_block(carry, items):
        rows, positive, named, mask, counts, cotangent = items
        qscale, qnorm = normalize(rows)
        scores = logit_scale * lax.dot_general(qnorm, pnorm, (((1,), (1,)), ((), ())), preferred_element_type=jnp.float32)
        valid = (mask == 1) & (slots[None, :] < counts[:, None])
        weights = weight_table(valid, named, pool_size)
        terms = weights * jnp.exp(scores)
        denom = lax.optimization_barrier(jnp.sum(terms, axis=1))
        chosen = columns[None, :] == positive[:, None]
        picked = lax.optimization_barrier(jnp.sum(jnp.where(chosen, scores, 0.0), axis=1))
        loss = jnp.log(denom) - picked
        coef = (logit_scale * cotangent[:, None] * (terms / denom[:, None] - chosen.astype(jnp.float32))).astype(jnp.bfloat16)
        qdir = jnp.dot(coef, pnorm, preferred_element_type=jnp.float32)
        grad_rows = tangent_back(rows, qscale, qdir)
        carry = carry + lax.dot_general(coef, qnorm, (((0,), (0,)), ((), ())), preferred_element_type=jnp.float32)
        return (carry, (loss, grad_rows))
    items = (queries.reshape(groups, QDEV, -1), pos_ids.reshape(groups, QDEV), neg_ids.reshape(groups, QDEV, NEG), neg_mask.reshape(groups, QDEV, NEG), neg_counts.reshape(groups, QDEV), d_loss.reshape(groups, QDEV))
    start = jnp.zeros((pool_size, passages.shape[1]), jnp.float32)
    pdir, (losses, grads) = lax.scan(one_block, start, items)
    grad_passages = tangent_back(passages, pscale, pdir)
    return (losses.reshape(-1), grads.reshape(queries.shape[0], -1), grad_passages)
```

```python
import jax
import jax.numpy as jnp
from jax import lax
from jax.sharding import PartitionSpec as P

logit_scale = 50.0
norm_eps = 1e-06


def stage_bits(size):
    bits = [1 << b for b in range(size.bit_length() - 1)][::-1]
    if len(bits) >= 4:
        return [bits[:2]] + [[b] for b in bits[2:]]
    return [[b] for b in bits]


def masks_of(bits):
    masks = [0]
    for b in bits:
        masks = masks + [m | b for m in masks]
    return masks


def swap(x, axis, size, mask):
    return lax.ppermute(x, axis, [(i, i ^ mask) for i in range(size)])


def row_scales(rows):
    wide = rows.astype(jnp.float32)
    return lax.rsqrt(jnp.sum(wide * wide, axis=-1) + norm_eps)


def weight_table(valid, neg_ids, columns):
    slots = neg_ids.shape[1]
    named = jnp.where(valid, neg_ids, -1)
    weights = jnp.ones((neg_ids.shape[0], columns.shape[0]), jnp.float32)
    for k in range(slots):
        weights = weights + (named[:, k : k + 1] == columns[None, :]).astype(jnp.float32)
    return weights


def make_local(loop, narrow):
    stages = stage_bits(loop)

    def local(queries, passages, pos_ids, neg_ids, neg_mask, neg_counts, d_loss):
        me = lax.axis_index("loop")
        block, width = passages.shape

        pool, order = passages[None], [0]
        for bits in stages:
            masks = masks_of(bits)
            pool = jnp.concatenate([pool] + [swap(pool, "loop", loop, m) for m in masks[1:]], axis=0)
            order = [o ^ m for m in masks for o in order]
        pool = pool.reshape(loop * block, width)
        owners = jnp.array(order, jnp.int32) ^ me
        columns = (owners[:, None] * block + jnp.arange(block, dtype=jnp.int32)[None, :]).reshape(-1)

        qscale = row_scales(queries)
        slots = jnp.arange(neg_ids.shape[1], dtype=jnp.int32)
        valid = (neg_mask == 1) & (slots[None, :] < neg_counts[:, None])
        weights = weight_table(valid, neg_ids, columns)

        pscale = row_scales(pool)
        raw = lax.dot_general(queries, pool, (((1,), (1,)), ((), ())), preferred_element_type=jnp.float32)
        cosine = raw * qscale[:, None] * pscale[None, :]
        scores = logit_scale * cosine
        terms = weights * jnp.exp(scores)
        denom = jnp.sum(terms, axis=1)
        chosen = columns[None, :] == pos_ids[:, None]
        picked = jnp.sum(jnp.where(chosen, scores, 0.0), axis=1)
        query_loss = jnp.log(denom) - picked
        coef = logit_scale * d_loss[:, None] * (terms / denom[:, None] - chosen.astype(jnp.float32))

        pcoef = (coef * qscale[:, None]).astype(jnp.bfloat16)
        total = lax.dot_general(pcoef, queries, (((0,), (0,)), ((), ())), preferred_element_type=jnp.float32)
        total = total.reshape(loop, block, width)
        for bits in stages[::-1]:
            masks = masks_of(bits)
            part = total.shape[0] // len(masks)
            sent = total[part:].astype(jnp.bfloat16)
            total = total[:part]
            for n, m in enumerate(masks[1:]):
                total = total + swap(sent[n * part : (n + 1) * part], "loop", loop, m).astype(jnp.float32)
        pdir = total[0]
        for b in range(narrow.bit_length() - 1):
            pdir = pdir + swap(pdir.astype(jnp.bfloat16), "narrow", narrow, 1 << b).astype(jnp.float32)

        qcoef = (coef * pscale[None, :]).astype(jnp.bfloat16)
        qdir = jnp.dot(qcoef, pool, preferred_element_type=jnp.float32)
        inner = jnp.sum(qcoef.astype(jnp.float32) * raw, axis=1) * qscale * qscale
        grad_queries = qscale[:, None] * (qdir - queries.astype(jnp.float32) * inner[:, None])

        own = row_scales(passages)
        punit = passages.astype(jnp.float32) * own[:, None]
        pinner = jnp.sum(punit * pdir, axis=-1, keepdims=True)
        grad_passages = own[:, None] * (pdir - punit * pinner)
        return query_loss, grad_queries.astype(jnp.bfloat16), grad_passages.astype(jnp.bfloat16)

    return local


def solution(mesh):
    return jax.shard_map(
        make_local(mesh.shape["loop"], mesh.shape["narrow"]),
        mesh=mesh,
        in_specs=(
            P(("loop", "narrow"), None),
            P("loop", None),
            P(("loop", "narrow")),
            P(("loop", "narrow"), None),
            P(("loop", "narrow"), None),
            P(("loop", "narrow")),
            P(("loop", "narrow")),
        ),
        out_specs=(P(("loop", "narrow")), P(("loop", "narrow"), None), P("loop", None)),
        check_vma=False,
    )
```

```python
import functools

import jax
import jax.numpy as jnp
from jax import lax
from jax.experimental import pallas as pl
from jax.experimental.pallas import tpu as pltpu
from jax.sharding import PartitionSpec as P

logit_scale = 50.0
norm_eps = 1e-06


VMEM = pl.BlockSpec(memory_space=pltpu.VMEM)
SMEM = pl.BlockSpec(memory_space=pltpu.SMEM)
ROWS = (((1,), (1,)), ((), ()))


def stage_bits(size):
    bits = [1 << b for b in range(size.bit_length() - 1)][::-1]
    return [bits[:2]] + [[b] for b in bits[2:]]


def masks_of(bits):
    masks = [0]
    for b in bits:
        masks = masks + [m | b for m in masks]
    return masks


def swap(x, axis, size, mask):
    return lax.ppermute(x, axis, [(i, i ^ mask) for i in range(size)])


def wide(x):
    return x.astype(jnp.float32)


LIMIT = pltpu.CompilerParams(vmem_limit_bytes=16 * 1024 * 1024)


def cost(flops, moved):
    return pl.CostEstimate(flops=flops, bytes_accessed=moved, transcendentals=0)


def passage_ids(order, block, shape, me):
    row = lax.broadcasted_iota(jnp.int32, shape, 0)
    place = row // block
    owner = jnp.full(shape, me, jnp.int32)
    for b in range(len(order).bit_length() - 1):
        owner = owner ^ (((place >> b) & 1) * order[1 << b])
    return owner * block + (row - place * block)


def weight_kernel(order, block, me_ref, ids_ref, mask_ref, count_ref, w_ref):
    slots = ids_ref.shape[0]
    slot = lax.broadcasted_iota(jnp.int32, ids_ref.shape, 0)
    named = jnp.where((mask_ref[...] == 1) & (slot < count_ref[...]), ids_ref[...], -1)
    columns = passage_ids(order, block, w_ref.shape, me_ref[0])
    weights = jnp.ones(w_ref.shape, jnp.float32)
    for k in range(slots):
        weights = weights + jnp.where(named[k : k + 1] == columns, 1.0, 0.0)
    w_ref[...] = weights


def raw_and_scale(refs, q):
    rows = jnp.concatenate([r[...] for r in refs], axis=0)
    f = wide(rows)
    scale = lax.rsqrt(jnp.sum(f * f, axis=1, keepdims=True) + norm_eps)
    return lax.dot_general(rows, q, ROWS, preferred_element_type=jnp.float32), scale


def first_kernel(n, *refs):
    q_ref, raw_ref, scale_ref = refs[n:]
    raw, scale = raw_and_scale(refs[:n], q_ref[...])
    raw_ref[...] = raw
    scale_ref[...] = jnp.broadcast_to(scale, scale_ref.shape)


def loss_kernel(n, order, block, *refs):
    me_ref, q_ref, rawa_ref, scalea_ref, w_ref, qs_ref, pos_ref, dl_ref = refs[n : n + 8]
    sent_ref, pa_ref, qc_ref, loss_ref, inner_ref = refs[n + 8 :]
    half = rawa_ref.shape[0]
    q = q_ref[...]
    qs = qs_ref[...]
    rawb, scaleb = raw_and_scale(refs[:n], q)
    raw = jnp.concatenate([rawa_ref[...], rawb], axis=0)
    scale = jnp.concatenate([scalea_ref[:, :1], scaleb], axis=0)
    scores = logit_scale * (raw * scale * qs)
    terms = w_ref[...] * jnp.exp(scores)
    denom = jnp.sum(terms, axis=0, keepdims=True)
    chosen = passage_ids(order, block, scores.shape, me_ref[0]) == pos_ref[...]
    coef = (logit_scale * dl_ref[...]) * (terms / denom - jnp.where(chosen, 1.0, 0.0))
    pcoef = (coef * qs).astype(jnp.bfloat16)
    sent_ref[...] = jnp.dot(pcoef[half:], q, preferred_element_type=jnp.float32).astype(jnp.bfloat16)
    pa_ref[...] = pcoef[:half]
    qcoef = (coef * scale).astype(jnp.bfloat16)
    qc_ref[...] = qcoef
    loss_ref[...] = jnp.log(denom) - jnp.sum(jnp.where(chosen, scores, 0.0), axis=0, keepdims=True)
    inner_ref[...] = jnp.sum(wide(qcoef) * raw, axis=0, keepdims=True) * qs * qs


def kept_kernel(pa_ref, q_ref, kept_ref):
    kept_ref[...] = jnp.dot(pa_ref[...], q_ref[...], preferred_element_type=jnp.float32)


def query_kernel(n, *refs):
    qc_ref, q_ref, qs_ref, inner_ref, out_ref = refs[n:]
    rows = jnp.concatenate([r[...] for r in refs[:n]], axis=0)
    qdir = lax.dot_general(qc_ref[...], rows, (((0,), (0,)), ((), ())), preferred_element_type=jnp.float32)
    out_ref[...] = (qs_ref[...] * (qdir - wide(q_ref[...]) * inner_ref[...])).astype(jnp.bfloat16)


def make_local(loop, narrow):
    stages = stage_bits(loop)

    def local(queries, passages, pos_ids, neg_ids, neg_mask, neg_counts, d_loss):
        me = lax.axis_index("loop")
        me_arr = me.astype(jnp.int32).reshape(1)
        block, width = passages.shape
        count = queries.shape[0]
        pool_size = loop * block

        pool, order = [passages], [0]
        for at, bits in enumerate(stages):
            masks = masks_of(bits)
            pool = pool + [swap(t, "loop", loop, m) for m in masks[1:] for t in pool]
            if at < len(stages) - 2:
                pool = [jnp.concatenate(pool, axis=0)]
            order = [o ^ m for m in masks for o in order]
        n = len(pool) // 2
        half = pool_size // 2

        wq = wide(queries)
        qscale = lax.rsqrt(jnp.sum(wq * wq, axis=-1) + norm_eps)
        qs = qscale.reshape(1, count)

        f32 = jnp.float32
        weights = pl.pallas_call(
            functools.partial(weight_kernel, order, block),
            out_shape=jax.ShapeDtypeStruct((pool_size, count), f32),
            in_specs=[SMEM, VMEM, VMEM, VMEM],
            out_specs=VMEM,
            cost_estimate=cost(10000000, 100000),
            compiler_params=LIMIT,
            name="weights",
        )(me_arr, neg_ids.T, neg_mask.T, neg_counts.reshape(1, count))
        rawa, scalea = pl.pallas_call(
            functools.partial(first_kernel, n),
            out_shape=(jax.ShapeDtypeStruct((half, count), f32), jax.ShapeDtypeStruct((half, 128), f32)),
            in_specs=[VMEM] * (n + 1),
            out_specs=(VMEM, VMEM),
            cost_estimate=cost(2 * half * count * width, 2000000),
            compiler_params=LIMIT,
            name="first_scores",
        )(*pool[:n], queries)
        sent, pa, qc, loss, inner = pl.pallas_call(
            functools.partial(loss_kernel, n, order, block),
            out_shape=(
                jax.ShapeDtypeStruct((half, width), jnp.bfloat16),
                jax.ShapeDtypeStruct((half, count), jnp.bfloat16),
                jax.ShapeDtypeStruct((pool_size, count), jnp.bfloat16),
                jax.ShapeDtypeStruct((1, count), f32),
                jax.ShapeDtypeStruct((1, count), f32),
            ),
            in_specs=[VMEM] * n + [SMEM] + [VMEM] * 7,
            out_specs=(VMEM,) * 5,
            cost_estimate=cost(4 * half * count * width, 2000000),
            compiler_params=LIMIT,
            name="loss",
        )(*pool[n:], me_arr, queries, rawa, scalea, weights, qs, pos_ids.reshape(1, count), d_loss.reshape(1, count))
        total = pl.pallas_call(
            kept_kernel,
            out_shape=jax.ShapeDtypeStruct((half, width), f32),
            in_specs=[VMEM] * 2,
            out_specs=VMEM,
            cost_estimate=cost(2 * half * count * width, 2000000),
            compiler_params=LIMIT,
            name="kept_terms",
        )(pa, queries)

        total = total + wide(swap(sent, "loop", loop, stages[-1][0]))
        for bits in stages[:-1][::-1]:
            masks = masks_of(bits)
            part = total.shape[0] // len(masks)
            sends = [total[k * part : (k + 1) * part].astype(jnp.bfloat16) for k in range(1, len(masks))]
            total = total[:part]
            for t, m in zip(sends, masks[1:]):
                total = total + wide(swap(t, "loop", loop, m))
        pdir = total
        for b in range(narrow.bit_length() - 1):
            pdir = pdir + wide(swap(pdir.astype(jnp.bfloat16), "narrow", narrow, 1 << b))

        step = 512
        column = lambda i: (0, i)
        fixed = lambda i: (0, 0)
        grad_queries = pl.pallas_call(
            functools.partial(query_kernel, 2 * n),
            out_shape=jax.ShapeDtypeStruct(queries.shape, jnp.bfloat16),
            grid=(width // step,),
            in_specs=[pl.BlockSpec((t.shape[0], step), column) for t in pool]
            + [
                pl.BlockSpec((pool_size, count), fixed),
                pl.BlockSpec((count, step), column),
                pl.BlockSpec((count, 1), fixed),
                pl.BlockSpec((count, 1), fixed),
            ],
            out_specs=pl.BlockSpec((count, step), column),
            cost_estimate=cost(2 * pool_size * count * width, 5000000),
            compiler_params=LIMIT,
            name="query_gradients",
        )(*pool, qc, queries, qscale.reshape(count, 1), inner.reshape(count, 1))

        wp = wide(passages)
        own = lax.rsqrt(jnp.sum(wp * wp, axis=-1, keepdims=True) + norm_eps)
        punit = wp * own
        pinner = jnp.sum(punit * pdir, axis=-1, keepdims=True)
        grad_passages = (own * (pdir - punit * pinner)).astype(jnp.bfloat16)
        return loss.reshape(count), grad_queries, grad_passages

    return local


def solution(mesh):
    return jax.shard_map(
        make_local(mesh.shape["loop"], mesh.shape["narrow"]),
        mesh=mesh,
        in_specs=(
            P(("loop", "narrow"), None),
            P("loop", None),
            P(("loop", "narrow")),
            P(("loop", "narrow"), None),
            P(("loop", "narrow"), None),
            P(("loop", "narrow")),
            P(("loop", "narrow")),
        ),
        out_specs=(P(("loop", "narrow")), P(("loop", "narrow"), None), P("loop", None)),
        check_vma=False,
    )
```

```python
import functools

import jax
import jax.numpy as jnp
from jax import lax
from jax.experimental import pallas as pl
from jax.experimental.pallas import tpu as pltpu
from jax.sharding import PartitionSpec as P


logit_scale = 50.0
norm_eps = 1e-06


VMEM = pl.BlockSpec(memory_space=pltpu.VMEM)
SMEM = pl.BlockSpec(memory_space=pltpu.SMEM)
ROWS = (((1,), (1,)), ((), ()))


def stage_masks(size):
    bits = [1 << b for b in range(size.bit_length() - 1)][::-1]
    first = [0, bits[1] | 1, bits[0] | 1, bits[0] | bits[1] | 1]
    return [first] + [[0, b | 1] for b in bits[2:]]


def swap(x, axis, size, mask):
    return lax.ppermute(x, axis, [(i, i ^ mask) for i in range(size)])


def wide(x):
    return x.astype(jnp.float32)


LIMIT = pltpu.CompilerParams(vmem_limit_bytes=16 * 1024 * 1024)
WIDE_LIMIT = pltpu.CompilerParams(vmem_limit_bytes=60 * 1024 * 1024)


def cost(flops, moved):
    return pl.CostEstimate(flops=flops, bytes_accessed=moved, transcendentals=0)


def passage_ids(stages, block, shape, me):
    row = lax.broadcasted_iota(jnp.int32, shape, 0)
    place = row // block
    digits, owner = place, jnp.full(shape, me, jnp.int32)
    for masks in stages:
        digit = digits % len(masks)
        digits = digits // len(masks)
        chosen = jnp.zeros(shape, jnp.int32)
        for k, m in enumerate(masks[1:]):
            chosen = jnp.where(digit == k + 1, m, chosen)
        owner = owner ^ chosen
    return owner * block + (row - place * block)


def prepare_kernel(
    stages, block, me_ref, ids_hbm, mask_hbm, count_hbm, q_hbm, w_ref, qs_ref, q_ref, ids_ref, mask_ref, count_ref, sems
):
    parts = sems.shape[0] - 3
    rows = q_ref.shape[0] // parts
    small = [
        pltpu.make_async_copy(src, dst, sems.at[parts + k])
        for k, (src, dst) in enumerate(((ids_hbm, ids_ref), (mask_hbm, mask_ref), (count_hbm, count_ref)))
    ]
    large = [
        pltpu.make_async_copy(q_hbm.at[pl.ds(k * rows, rows)], q_ref.at[pl.ds(k * rows, rows)], sems.at[k])
        for k in range(parts)
    ]
    for copy in small + large:
        copy.start()
    columns = passage_ids(stages, block, w_ref.shape, me_ref[0])
    for copy in small:
        copy.wait()
    slots = ids_ref.shape[0]
    slot = lax.broadcasted_iota(jnp.int32, ids_ref.shape, 0)
    named = jnp.where((mask_ref[...] == 1) & (slot < count_ref[...]), ids_ref[...], -1)
    weights = jnp.ones(w_ref.shape, jnp.float32)
    for k in range(slots):
        weights = weights + jnp.where(named[k : k + 1] == columns, 1.0, 0.0)
    w_ref[...] = weights
    scales = []
    for k in range(parts):
        large[k].wait()
        f = wide(q_ref[k * rows : (k + 1) * rows])
        scales.append(lax.rsqrt(jnp.sum(f * f, axis=1, keepdims=True) + norm_eps))
    scale = jnp.concatenate(scales, axis=0)
    qs_ref[...] = jnp.broadcast_to(scale, (scale.shape[0], 128)).T[:1]


def raw_and_scale(refs, q):
    rows = jnp.concatenate([r[...] for r in refs], axis=0)
    f = wide(rows)
    scale = lax.rsqrt(jnp.sum(f * f, axis=1, keepdims=True) + norm_eps)
    return lax.dot_general(rows, q, ROWS, preferred_element_type=jnp.float32), scale


def first_kernel(n, *refs):
    q_ref, raw_ref, scale_ref = refs[n:]
    raw, scale = raw_and_scale(refs[:n], q_ref[...])
    raw_ref[...] = raw
    scale_ref[...] = jnp.broadcast_to(scale, scale_ref.shape)


def loss_kernel(n, stages, block, *refs):
    me_ref, q_ref, rawa_ref, scalea_ref, w_ref, qs_ref, pos_ref, dl_ref = refs[n : n + 8]
    sent_ref, pa_ref, qc_ref, loss_ref, inner_ref = refs[n + 8 :]
    half = rawa_ref.shape[0]
    q = q_ref[...]
    qs = qs_ref[...]
    rawb, scaleb = raw_and_scale(refs[:n], q)
    raw = jnp.concatenate([rawa_ref[...], rawb], axis=0)
    scale = jnp.concatenate([scalea_ref[:, :1], scaleb], axis=0)
    scores = logit_scale * (raw * scale * qs)
    terms = w_ref[...] * jnp.exp(scores)
    denom = jnp.sum(terms, axis=0, keepdims=True)
    chosen = passage_ids(stages, block, scores.shape, me_ref[0]) == pos_ref[...]
    coef = (logit_scale * dl_ref[...]) * (terms / denom - jnp.where(chosen, 1.0, 0.0))
    pcoef = (coef * qs).astype(jnp.bfloat16)
    sent_ref[...] = jnp.dot(pcoef[half:], q, preferred_element_type=jnp.float32).astype(jnp.bfloat16)
    pa_ref[...] = pcoef[:half]
    qcoef = (coef * qs * scale).astype(jnp.bfloat16)
    qc_ref[...] = qcoef
    loss_ref[...] = jnp.log(denom) - jnp.sum(jnp.where(chosen, scores, 0.0), axis=0, keepdims=True)
    inner_ref[...] = jnp.sum(wide(qcoef) * raw, axis=0, keepdims=True) * qs * qs


def kept_kernel(pa_ref, q_ref, kept_ref):
    kept_ref[...] = jnp.dot(pa_ref[...], q_ref[...], preferred_element_type=jnp.float32)


def query_kernel(n, *refs):
    qc_ref, q_ref, inner_ref, out_ref = refs[n:]
    step = out_ref.shape[1]
    at = pl.ds(pl.multiple_of(pl.program_id(0) * step, step), step)
    rows = jnp.concatenate([r[:, at] for r in refs[:n]], axis=0)
    qdir = lax.dot_general(qc_ref[...], rows, (((0,), (0,)), ((), ())), preferred_element_type=jnp.float32)
    inner = jnp.broadcast_to(inner_ref[...], (128, inner_ref.shape[1])).T[:, :1]
    out_ref[...] = (qdir - wide(q_ref[:, at]) * inner).astype(jnp.bfloat16)


def passage_kernel(n, p_ref, total_ref, *refs):
    out_ref = refs[n]
    pdir = total_ref[...]
    for r in refs[:n]:
        pdir = pdir + wide(r[...])
    f = wide(p_ref[...])
    scale = lax.rsqrt(jnp.sum(f * f, axis=1, keepdims=True) + norm_eps)
    unit = f * scale
    inner = jnp.sum(unit * pdir, axis=1, keepdims=True)
    out_ref[...] = (scale * (pdir - unit * inner)).astype(jnp.bfloat16)


def make_local(loop, narrow):
    stages = stage_masks(loop)

    def local(queries, passages, pos_ids, neg_ids, neg_mask, neg_counts, d_loss):
        return body(queries, passages, pos_ids, neg_ids, neg_mask, neg_counts, d_loss)

    def body(queries, passages, pos_ids, neg_ids, neg_mask, neg_counts, d_loss):
        me = lax.axis_index("loop")
        me_arr = me.astype(jnp.int32).reshape(1)
        block, width = passages.shape
        count = queries.shape[0]
        pool_size = loop * block

        first = [passages] + [swap(passages, "loop", loop, m) for m in stages[0][1:]]
        pool = [jnp.concatenate(first[k : k + 2], axis=0) for k in (0, 2)]
        for at, (_, m) in enumerate(stages[1:]):
            moved = [swap(t, "loop", loop, m) for t in pool]
            pool = pool + moved
            if at < len(stages) - 3:
                pool = [jnp.concatenate(pool, axis=0)]
        n = len(pool) // 2
        half = pool_size // 2

        f32 = jnp.float32
        parts = 4
        weights, qs = pl.pallas_call(
            functools.partial(prepare_kernel, stages, block),
            out_shape=(
                jax.ShapeDtypeStruct((pool_size, count), f32),
                jax.ShapeDtypeStruct((1, count), f32),
            ),
            in_specs=[SMEM] + [pl.BlockSpec(memory_space=pltpu.HBM)] * 4,
            out_specs=(VMEM,) * 2,
            scratch_shapes=[
                pltpu.VMEM(queries.shape, queries.dtype),
                pltpu.VMEM(neg_ids.shape[::-1], jnp.int32),
                pltpu.VMEM(neg_ids.shape[::-1], jnp.int32),
                pltpu.VMEM((1, count), jnp.int32),
                pltpu.SemaphoreType.DMA((parts + 3,)),
            ],
            cost_estimate=cost(10000000, 3000000),
            compiler_params=WIDE_LIMIT,
            name="prepare",
        )(me_arr, neg_ids.T, neg_mask.T, neg_counts.reshape(1, count), queries)
        rawa, scalea = pl.pallas_call(
            functools.partial(first_kernel, n),
            out_shape=(jax.ShapeDtypeStruct((half, count), f32), jax.ShapeDtypeStruct((half, 128), f32)),
            in_specs=[VMEM] * (n + 1),
            out_specs=(VMEM, VMEM),
            cost_estimate=cost(2 * half * count * width, 2000000),
            compiler_params=LIMIT,
            name="first_scores",
        )(*pool[:n], queries)
        sent, pa, qc, loss, inner = pl.pallas_call(
            functools.partial(loss_kernel, n, stages, block),
            out_shape=(
                jax.ShapeDtypeStruct((half, width), jnp.bfloat16),
                jax.ShapeDtypeStruct((half, count), jnp.bfloat16),
                jax.ShapeDtypeStruct((pool_size, count), jnp.bfloat16),
                jax.ShapeDtypeStruct((1, count), f32),
                jax.ShapeDtypeStruct((1, count), f32),
            ),
            in_specs=[VMEM] * n + [SMEM] + [VMEM] * 7,
            out_specs=(VMEM,) * 5,
            cost_estimate=cost(4 * half * count * width, 2000000),
            compiler_params=LIMIT,
            name="loss",
        )(*pool[n:], me_arr, queries, rawa, scalea, weights, qs, pos_ids.reshape(1, count), d_loss.reshape(1, count))
        total = pl.pallas_call(
            kept_kernel,
            out_shape=jax.ShapeDtypeStruct((half, width), f32),
            in_specs=[VMEM] * 2,
            out_specs=VMEM,
            cost_estimate=cost(2 * half * count * width, 2000000),
            compiler_params=LIMIT,
            name="kept_terms",
        )(pa, queries)

        total = total + wide(swap(sent, "loop", loop, stages[-1][1]))
        for masks in stages[:-1][::-1]:
            part = total.shape[0] // len(masks)
            moved = [
                swap(total[k * part : (k + 1) * part].astype(jnp.bfloat16), "loop", loop, masks[k])
                for k in range(len(masks) - 1, 0, -1)
            ]
            total = total[:part]
            for t in moved:
                total = total + wide(t)
        moved = []
        for b in range(narrow.bit_length() - 1):
            if moved:
                total = total + wide(moved.pop())
            moved.append(swap(total.astype(jnp.bfloat16), "narrow", narrow, 1 << b))

        step = 512
        grad_queries = pl.pallas_call(
            functools.partial(query_kernel, 2 * n),
            out_shape=jax.ShapeDtypeStruct(queries.shape, jnp.bfloat16),
            grid=(width // step,),
            in_specs=[VMEM] * (2 * n + 3),
            out_specs=pl.BlockSpec((count, step), lambda i: (0, i)),
            cost_estimate=cost(2 * pool_size * count * width, 5000000),
            compiler_params=LIMIT,
            name="query_gradients",
        )(*pool, qc, queries, inner)
        grad_passages = pl.pallas_call(
            functools.partial(passage_kernel, len(moved)),
            out_shape=jax.ShapeDtypeStruct(passages.shape, jnp.bfloat16),
            in_specs=[VMEM] * (2 + len(moved)),
            out_specs=VMEM,
            cost_estimate=cost(1000000, 200000),
            compiler_params=LIMIT,
            name="passage_gradients",
        )(passages, total, *moved)
        return loss.reshape(count), grad_queries, grad_passages

    return local


def solution(mesh):
    return jax.shard_map(
        make_local(mesh.shape["loop"], mesh.shape["narrow"]),
        mesh=mesh,
        in_specs=(
            P(("loop", "narrow"), None),
            P("loop", None),
            P(("loop", "narrow")),
            P(("loop", "narrow"), None),
            P(("loop", "narrow"), None),
            P(("loop", "narrow")),
            P(("loop", "narrow")),
        ),
        out_specs=(P(("loop", "narrow")), P(("loop", "narrow"), None), P("loop", None)),
        check_vma=False,
    )
```

```python
import functools

import jax
import jax.numpy as jnp
from jax import lax
from jax.experimental import pallas as pl
from jax.experimental.pallas import tpu as pltpu
from jax.sharding import PartitionSpec as P


logit_scale = 50.0
norm_eps = 1e-06


VMEM = pl.BlockSpec(memory_space=pltpu.VMEM)
SMEM = pl.BlockSpec(memory_space=pltpu.SMEM)
ROWS = (((1,), (1,)), ((), ()))


def stage_masks(size):
    bits = [1 << b for b in range(size.bit_length() - 1)][::-1]
    first = [0, bits[1] | 1, bits[0] | 1, bits[0] | bits[1] | 1]
    return [first] + [[0, b | 1] for b in bits[2:]]


def swap(x, axis, size, mask):
    return lax.ppermute(x, axis, [(i, i ^ mask) for i in range(size)])


def wide(x):
    return x.astype(jnp.float32)


LIMIT = pltpu.CompilerParams(vmem_limit_bytes=16 * 1024 * 1024)
WIDE_LIMIT = pltpu.CompilerParams(vmem_limit_bytes=60 * 1024 * 1024)


def cost(flops, moved):
    return pl.CostEstimate(flops=flops, bytes_accessed=moved, transcendentals=0)


def passage_ids(stages, block, shape, me):
    row = lax.broadcasted_iota(jnp.int32, shape, 0)
    place = row // block
    digits, owner = place, jnp.full(shape, me, jnp.int32)
    for masks in stages:
        digit = digits % len(masks)
        digits = digits // len(masks)
        chosen = jnp.zeros(shape, jnp.int32)
        for k, m in enumerate(masks[1:]):
            chosen = jnp.where(digit == k + 1, m, chosen)
        owner = owner ^ chosen
    return owner * block + (row - place * block)


def prepare_kernel(
    stages, block, me_ref, ids_hbm, mask_hbm, count_hbm, q_hbm, w_ref, qs_ref, q_ref, ids_ref, mask_ref, count_ref, sems
):
    parts = sems.shape[0] - 3
    rows = q_ref.shape[0] // parts
    small = [
        pltpu.make_async_copy(src, dst, sems.at[parts + k])
        for k, (src, dst) in enumerate(((ids_hbm, ids_ref), (mask_hbm, mask_ref), (count_hbm, count_ref)))
    ]
    large = [
        pltpu.make_async_copy(q_hbm.at[pl.ds(k * rows, rows)], q_ref.at[pl.ds(k * rows, rows)], sems.at[k])
        for k in range(parts)
    ]
    for copy in small + large:
        copy.start()
    columns = passage_ids(stages, block, w_ref.shape, me_ref[0])
    for copy in small:
        copy.wait()
    slots = ids_ref.shape[0]
    slot = lax.broadcasted_iota(jnp.int32, ids_ref.shape, 0)
    named = jnp.where((mask_ref[...] == 1) & (slot < count_ref[...]), ids_ref[...], -1)
    weights = jnp.ones(w_ref.shape, jnp.float32)
    for k in range(slots):
        weights = weights + jnp.where(named[k : k + 1] == columns, 1.0, 0.0)
    w_ref[...] = weights
    scales = []
    for k in range(parts):
        large[k].wait()
        f = wide(q_ref[k * rows : (k + 1) * rows])
        scales.append(lax.rsqrt(jnp.sum(f * f, axis=1, keepdims=True) + norm_eps))
    scale = jnp.concatenate(scales, axis=0)
    qs_ref[...] = jnp.broadcast_to(scale, (scale.shape[0], 128)).T[:1]


def raw_and_scale(refs, q):
    rows = jnp.concatenate([r[...] for r in refs], axis=0)
    f = wide(rows)
    scale = lax.rsqrt(jnp.sum(f * f, axis=1, keepdims=True) + norm_eps)
    return lax.dot_general(rows, q, ROWS, preferred_element_type=jnp.float32), scale


def first_kernel(n, *refs):
    q_ref, raw_ref, scale_ref = refs[n:]
    raw, scale = raw_and_scale(refs[:n], q_ref[...])
    raw_ref[...] = raw
    scale_ref[...] = jnp.broadcast_to(scale, scale_ref.shape)


def loss_kernel(n, stages, block, *refs):
    me_ref, q_ref, rawa_ref, scalea_ref, w_ref, qs_ref, pos_ref, dl_ref = refs[n : n + 8]
    sent_ref, pa_ref, qc_ref, loss_ref, inner_ref = refs[n + 8 :]
    half = rawa_ref.shape[0]
    q = q_ref[...]
    qs = qs_ref[...]
    rawb, scaleb = raw_and_scale(refs[:n], q)
    raw = jnp.concatenate([rawa_ref[...], rawb], axis=0)
    scale = jnp.concatenate([scalea_ref[:, :1], scaleb], axis=0)
    scores = logit_scale * (raw * scale * qs)
    terms = w_ref[...] * jnp.exp(scores)
    denom = jnp.sum(terms, axis=0, keepdims=True)
    chosen = passage_ids(stages, block, scores.shape, me_ref[0]) == pos_ref[...]
    coef = (logit_scale * dl_ref[...]) * (terms / denom - jnp.where(chosen, 1.0, 0.0))
    pcoef = (coef * qs).astype(jnp.bfloat16)
    sent_ref[...] = jnp.dot(pcoef[half:], q, preferred_element_type=jnp.float32).astype(jnp.bfloat16)
    pa_ref[...] = pcoef[:half]
    qcoef = (coef * qs * scale).astype(jnp.bfloat16)
    qc_ref[...] = qcoef
    loss_ref[...] = jnp.log(denom) - jnp.sum(jnp.where(chosen, scores, 0.0), axis=0, keepdims=True)
    inner_ref[...] = jnp.sum(wide(qcoef) * raw, axis=0, keepdims=True) * qs * qs


def kept_kernel(pa_ref, q_ref, kept_ref):
    kept_ref[...] = jnp.dot(pa_ref[...], q_ref[...], preferred_element_type=jnp.float32)


def split_kernel(total_ref, got_ref, kept0_ref, kept1_ref, sent0_ref, sent1_ref):
    total = total_ref[...] + wide(got_ref[...])
    part = kept0_ref.shape[0]
    for k, ref in enumerate((kept0_ref, kept1_ref, sent0_ref, sent1_ref)):
        ref[...] = total[k * part : (k + 1) * part].astype(ref.dtype)


def far_kernel(kept_ref, got_ref, low_ref, high_ref):
    total = kept_ref[...] + wide(got_ref[...])
    part = low_ref.shape[0]
    low_ref[...] = total[:part].astype(low_ref.dtype)
    high_ref[...] = total[part:].astype(high_ref.dtype)


def sum_call(kernel, outs, *args):
    return pl.pallas_call(
        kernel,
        out_shape=tuple(jax.ShapeDtypeStruct(*out) for out in outs),
        in_specs=[VMEM] * len(args),
        out_specs=(VMEM,) * len(outs),
        cost_estimate=cost(200000, 1000000),
        compiler_params=LIMIT,
    )(*args)


def query_kernel(n, first, *refs):
    qc_ref, q_ref, inner_ref = refs[n : n + 3]
    out_ref, coef_ref, column_ref = refs[-3:]
    step = out_ref.shape[1]

    @pl.when(pl.program_id(0) == 0)
    def _():
        coef_ref[...] = qc_ref[...].T
        column_ref[...] = jnp.broadcast_to(inner_ref[...], (128, inner_ref.shape[1])).T

    at = pl.ds(pl.multiple_of((first + pl.program_id(0)) * step, step), step)
    rows = jnp.concatenate([r[:, at] for r in refs[:n]], axis=0)
    qdir = jnp.dot(coef_ref[...], rows, preferred_element_type=jnp.float32)
    out_ref[...] = (qdir - wide(q_ref[:, at]) * column_ref[:, :1]).astype(jnp.bfloat16)


def passage_kernel(n, p_ref, total_ref, *refs):
    out_ref = refs[n]
    pdir = total_ref[...]
    for r in refs[:n]:
        pdir = pdir + wide(r[...])
    f = wide(p_ref[...])
    scale = lax.rsqrt(jnp.sum(f * f, axis=1, keepdims=True) + norm_eps)
    unit = f * scale
    inner = jnp.sum(unit * pdir, axis=1, keepdims=True)
    out_ref[...] = (scale * (pdir - unit * inner)).astype(jnp.bfloat16)


def make_local(loop, narrow):
    stages = stage_masks(loop)

    def local(queries, passages, pos_ids, neg_ids, neg_mask, neg_counts, d_loss):
        return body(queries, passages, pos_ids, neg_ids, neg_mask, neg_counts, d_loss)

    def body(queries, passages, pos_ids, neg_ids, neg_mask, neg_counts, d_loss):
        me = lax.axis_index("loop")
        me_arr = me.astype(jnp.int32).reshape(1)
        block, width = passages.shape
        count = queries.shape[0]
        pool_size = loop * block

        first = [passages] + [swap(passages, "loop", loop, m) for m in stages[0][1:]]
        pool = []
        for k in (0, 2):
            pool.append(jnp.concatenate(first[k : k + 2], axis=0))
        for at, (_, m) in enumerate(stages[1:]):
            moved = [swap(t, "loop", loop, m) for t in pool]
            pool = pool + moved
            if at < len(stages) - 3:
                pool = [jnp.concatenate(pool, axis=0)]
        n = len(pool) // 2
        half = pool_size // 2

        f32 = jnp.float32
        parts = 4
        weights, qs = pl.pallas_call(
            functools.partial(prepare_kernel, stages, block),
            out_shape=(
                jax.ShapeDtypeStruct((pool_size, count), f32),
                jax.ShapeDtypeStruct((1, count), f32),
            ),
            in_specs=[SMEM] + [pl.BlockSpec(memory_space=pltpu.HBM)] * 4,
            out_specs=(VMEM,) * 2,
            scratch_shapes=[
                pltpu.VMEM(queries.shape, queries.dtype),
                pltpu.VMEM(neg_ids.shape[::-1], jnp.int32),
                pltpu.VMEM(neg_ids.shape[::-1], jnp.int32),
                pltpu.VMEM((1, count), jnp.int32),
                pltpu.SemaphoreType.DMA((parts + 3,)),
            ],
            cost_estimate=cost(10000000, 3000000),
            compiler_params=WIDE_LIMIT,
            name="prepare",
        )(me_arr, neg_ids.T, neg_mask.T, neg_counts.reshape(1, count), queries)
        rawa, scalea = pl.pallas_call(
            functools.partial(first_kernel, n),
            out_shape=(jax.ShapeDtypeStruct((half, count), f32), jax.ShapeDtypeStruct((half, 128), f32)),
            in_specs=[VMEM] * (n + 1),
            out_specs=(VMEM, VMEM),
            cost_estimate=cost(2 * half * count * width, 2000000),
            compiler_params=LIMIT,
            name="first_scores",
        )(*pool[:n], queries)
        sent, pa, qc, loss, inner = pl.pallas_call(
            functools.partial(loss_kernel, n, stages, block),
            out_shape=(
                jax.ShapeDtypeStruct((half, width), jnp.bfloat16),
                jax.ShapeDtypeStruct((half, count), jnp.bfloat16),
                jax.ShapeDtypeStruct((pool_size, count), jnp.bfloat16),
                jax.ShapeDtypeStruct((1, count), f32),
                jax.ShapeDtypeStruct((1, count), f32),
            ),
            in_specs=[VMEM] * n + [SMEM] + [VMEM] * 7,
            out_specs=(VMEM,) * 5,
            cost_estimate=cost(4 * half * count * width, 2000000),
            compiler_params=LIMIT,
            name="loss",
        )(*pool[n:], me_arr, queries, rawa, scalea, weights, qs, pos_ids.reshape(1, count), d_loss.reshape(1, count))
        total = pl.pallas_call(
            kept_kernel,
            out_shape=jax.ShapeDtypeStruct((half, width), f32),
            in_specs=[VMEM] * 2,
            out_specs=VMEM,
            cost_estimate=cost(2 * half * count * width, 2000000),
            compiler_params=LIMIT,
            name="kept_terms",
        )(pa, queries)

        received = swap(sent, "loop", loop, stages[-1][1])
        for _, m in stages[2:-1][::-1]:
            total = total + wide(received)
            part = total.shape[0] // 2
            received = swap(total[part:].astype(jnp.bfloat16), "loop", loop, m)
            total = total[:part]
        part = total.shape[0] // 4
        kept0, kept1, sent0, sent1 = sum_call(
            split_kernel, [((part, width), f32)] * 2 + [((part, width), jnp.bfloat16)] * 2, total, received
        )
        got1 = swap(sent1, "loop", loop, stages[1][1])
        got0 = swap(sent0, "loop", loop, stages[1][1])
        term = ((block, width), jnp.bfloat16)
        far2, far3 = sum_call(far_kernel, [term, term], kept1, got1)
        got3 = swap(far3, "loop", loop, stages[0][3])
        got2 = swap(far2, "loop", loop, stages[0][2])
        total, far1 = sum_call(far_kernel, [((block, width), f32), term], kept0, got0)
        got1 = swap(far1, "loop", loop, stages[0][1])
        total = total + wide(got1) + wide(got2) + wide(got3)
        moved = []
        for b in range(narrow.bit_length() - 1):
            if moved:
                total = total + wide(moved.pop())
            moved.append(swap(total.astype(jnp.bfloat16), "narrow", narrow, 1 << b))

        step = 512
        calls = 2
        steps = width // step // calls
        grad_queries = None
        for k in range(calls):
            before = [] if grad_queries is None else [grad_queries]
            grad_queries = pl.pallas_call(
                functools.partial(query_kernel, 2 * n, k * steps),
                out_shape=jax.ShapeDtypeStruct(queries.shape, jnp.bfloat16),
                grid=(steps,),
                in_specs=[VMEM] * (2 * n + 3) + [pl.BlockSpec(memory_space=pl.ANY)] * len(before),
                out_specs=pl.BlockSpec((count, step), lambda i, k=k: (0, i + k * steps)),
                input_output_aliases={2 * n + 3: 0} if before else {},
                scratch_shapes=[pltpu.VMEM((count, pool_size), jnp.bfloat16), pltpu.VMEM((count, 128), f32)],
                cost_estimate=cost(2 * pool_size * count * width // calls, 5000000 // calls),
                compiler_params=LIMIT,
            )(*pool, qc, queries, inner, *before)
        grad_passages = pl.pallas_call(
            functools.partial(passage_kernel, len(moved)),
            out_shape=jax.ShapeDtypeStruct(passages.shape, jnp.bfloat16),
            in_specs=[VMEM] * (2 + len(moved)),
            out_specs=VMEM,
            cost_estimate=cost(1000000, 200000),
            compiler_params=LIMIT,
            name="passage_gradients",
        )(passages, total, *moved)
        return loss.reshape(count), grad_queries, grad_passages

    return local


def solution(mesh):
    return jax.shard_map(
        make_local(mesh.shape["loop"], mesh.shape["narrow"]),
        mesh=mesh,
        in_specs=(
            P(("loop", "narrow"), None),
            P("loop", None),
            P(("loop", "narrow")),
            P(("loop", "narrow"), None),
            P(("loop", "narrow"), None),
            P(("loop", "narrow")),
            P(("loop", "narrow")),
        ),
        out_specs=(P(("loop", "narrow")), P(("loop", "narrow"), None), P("loop", None)),
        check_vma=False,
    )
```

```python
import functools

import jax
import jax.numpy as jnp
from jax import lax
from jax.experimental import pallas as pl
from jax.experimental.pallas import tpu as pltpu
from jax.sharding import PartitionSpec as P


logit_scale = 50.0
norm_eps = 1e-06


VMEM = pl.BlockSpec(memory_space=pltpu.VMEM)
SMEM = pl.BlockSpec(memory_space=pltpu.SMEM)
ROWS = (((1,), (1,)), ((), ()))


def stage_masks(size):
    bits = [1 << b for b in range(size.bit_length() - 1)][::-1]
    first = [0, bits[1] | 1, bits[0] | 1, bits[0] | bits[1] | 1]
    return [first] + [[0, b | 1] for b in bits[2:]]


def swap(x, axis, size, mask):
    return lax.ppermute(x, axis, [(i, i ^ mask) for i in range(size)])


def wide(x):
    return x.astype(jnp.float32)


LIMIT = pltpu.CompilerParams(vmem_limit_bytes=16 * 1024 * 1024)
WIDE_LIMIT = pltpu.CompilerParams(vmem_limit_bytes=60 * 1024 * 1024)


def cost(flops, moved):
    return pl.CostEstimate(flops=flops, bytes_accessed=moved, transcendentals=0)


def passage_ids(stages, block, shape, me):
    row = lax.broadcasted_iota(jnp.int32, shape, 0)
    place = row // block
    digits, owner = place, jnp.full(shape, me, jnp.int32)
    for masks in stages:
        digit = digits % len(masks)
        digits = digits // len(masks)
        chosen = jnp.zeros(shape, jnp.int32)
        for k, m in enumerate(masks[1:]):
            chosen = jnp.where(digit == k + 1, m, chosen)
        owner = owner ^ chosen
    return owner * block + (row - place * block)


def weight_kernel(
    stages, block, me_ref, ids_hbm, mask_hbm, count_hbm, unused_hbm, w_ref, ids_ref, mask_ref, count_ref, sems
):
    copies = [
        pltpu.make_async_copy(src, dst, sems.at[k])
        for k, (src, dst) in enumerate(((ids_hbm, ids_ref), (mask_hbm, mask_ref), (count_hbm, count_ref)))
    ]
    for copy in copies:
        copy.start()
    columns = passage_ids(stages, block, w_ref.shape, me_ref[0])
    for copy in copies:
        copy.wait()
    slots = ids_ref.shape[0]
    slot = lax.broadcasted_iota(jnp.int32, ids_ref.shape, 0)
    named = jnp.where((mask_ref[...] == 1) & (slot < count_ref[...]), ids_ref[...], -1)
    weights = jnp.ones(w_ref.shape, jnp.float32)
    for k in range(slots):
        weights = weights + jnp.where(named[k : k + 1] == columns, 1.0, 0.0)
    w_ref[...] = weights


def raw_and_scale(refs, q):
    rows = jnp.concatenate([r[...] for r in refs], axis=0)
    f = wide(rows)
    scale = lax.rsqrt(jnp.sum(f * f, axis=1, keepdims=True) + norm_eps)
    return lax.dot_general(rows, q, ROWS, preferred_element_type=jnp.float32), scale


def early_kernel(n, *refs):
    q_ref, raw_ref, scale_ref, qs_ref = refs[n:]
    q = q_ref[...]
    raw, scale = raw_and_scale(refs[:n], q)
    raw_ref[...] = raw
    scale_ref[...] = jnp.broadcast_to(scale, scale_ref.shape)
    f = wide(q)
    own = lax.rsqrt(jnp.sum(f * f, axis=1, keepdims=True) + norm_eps)
    qs_ref[...] = jnp.broadcast_to(own, (own.shape[0], 128)).T[:1]


def interleave(first, second):
    part = first.shape[0] // 2
    return jnp.concatenate([first[:part], second[:part], first[part:], second[part:]], axis=0)


def loss_kernel(n, stages, block, *refs):
    me_ref, q_ref, rawa_ref, scalea_ref, w_ref, qs_ref, pos_ref, dl_ref = refs[n : n + 8]
    sent_ref, pa_ref, qc_ref, loss_ref, inner_ref = refs[n + 8 :]
    half = rawa_ref.shape[0]
    q = q_ref[...]
    qs = qs_ref[...]
    rawb, scaleb = raw_and_scale(refs[:n], q)
    raw = interleave(rawa_ref[...], rawb)
    scale = interleave(scalea_ref[:, :1], scaleb)
    scores = logit_scale * (raw * scale * qs)
    terms = w_ref[...] * jnp.exp(scores)
    denom = jnp.sum(terms, axis=0, keepdims=True)
    chosen = passage_ids(stages, block, scores.shape, me_ref[0]) == pos_ref[...]
    coef = (logit_scale * dl_ref[...]) * (terms / denom - jnp.where(chosen, 1.0, 0.0))
    pcoef = (coef * qs).astype(jnp.bfloat16)
    sent_ref[...] = jnp.dot(pcoef[half:], q, preferred_element_type=jnp.float32).astype(jnp.bfloat16)
    pa_ref[...] = pcoef[:half]
    qcoef = (coef * qs * scale).astype(jnp.bfloat16)
    qc_ref[...] = qcoef
    loss_ref[...] = jnp.log(denom) - jnp.sum(jnp.where(chosen, scores, 0.0), axis=0, keepdims=True)
    inner_ref[...] = jnp.sum(wide(qcoef) * raw, axis=0, keepdims=True) * qs * qs


def kept_kernel(pa_ref, q_ref, kept_ref):
    kept_ref[...] = jnp.dot(pa_ref[...], q_ref[...], preferred_element_type=jnp.float32)


def split_kernel(total_ref, got_ref, kept0_ref, kept1_ref, sent0_ref, sent1_ref):
    total = total_ref[...] + wide(got_ref[...])
    part = kept0_ref.shape[0]
    for k, ref in enumerate((kept0_ref, kept1_ref, sent0_ref, sent1_ref)):
        ref[...] = total[k * part : (k + 1) * part].astype(ref.dtype)


def far_kernel(kept_ref, got_ref, low_ref, high_ref):
    total = kept_ref[...] + wide(got_ref[...])
    part = low_ref.shape[0]
    low_ref[...] = total[:part].astype(low_ref.dtype)
    high_ref[...] = total[part:].astype(high_ref.dtype)


def sum_call(kernel, outs, *args):
    return pl.pallas_call(
        kernel,
        out_shape=tuple(jax.ShapeDtypeStruct(*out) for out in outs),
        in_specs=[VMEM] * len(args),
        out_specs=(VMEM,) * len(outs),
        cost_estimate=cost(200000, 1000000),
        compiler_params=LIMIT,
    )(*args)


def query_kernel(n, first, *refs):
    qc_ref, q_ref, inner_ref = refs[n : n + 3]
    out_ref, coef_ref, column_ref = refs[-3:]
    step = out_ref.shape[1]

    @pl.when(pl.program_id(0) == 0)
    def _():
        coef_ref[...] = qc_ref[...].T
        column_ref[...] = jnp.broadcast_to(inner_ref[...], (128, inner_ref.shape[1])).T

    at = pl.ds(pl.multiple_of((first + pl.program_id(0)) * step, step), step)
    rows = jnp.concatenate([r[:, at] for r in refs[:n]], axis=0)
    qdir = jnp.dot(coef_ref[...], rows, preferred_element_type=jnp.float32)
    out_ref[...] = (qdir - wide(q_ref[:, at]) * column_ref[:, :1]).astype(jnp.bfloat16)


def passage_kernel(n, p_ref, total_ref, *refs):
    out_ref = refs[n]
    pdir = total_ref[...]
    for r in refs[:n]:
        pdir = pdir + wide(r[...])
    f = wide(p_ref[...])
    scale = lax.rsqrt(jnp.sum(f * f, axis=1, keepdims=True) + norm_eps)
    unit = f * scale
    inner = jnp.sum(unit * pdir, axis=1, keepdims=True)
    out_ref[...] = (scale * (pdir - unit * inner)).astype(jnp.bfloat16)


def make_local(loop, narrow):
    stages = stage_masks(loop)

    def local(queries, passages, pos_ids, neg_ids, neg_mask, neg_counts, d_loss):
        return body(queries, passages, pos_ids, neg_ids, neg_mask, neg_counts, d_loss)

    def body(queries, passages, pos_ids, neg_ids, neg_mask, neg_counts, d_loss):
        me = lax.axis_index("loop")
        me_arr = me.astype(jnp.int32).reshape(1)
        block, width = passages.shape
        count = queries.shape[0]
        pool_size = loop * block

        first = [passages] + [swap(passages, "loop", loop, m) for m in stages[0][1:]]
        pool = []
        for k in (0, 2):
            pool.append(jnp.concatenate(first[k : k + 2], axis=0))
        for at, (_, m) in enumerate(stages[1:]):
            moved = [swap(t, "loop", loop, m) for t in pool]
            pool = pool + moved
            if at < len(stages) - 3:
                pool = [jnp.concatenate(pool, axis=0)]
        n = len(pool) // 2
        half = pool_size // 2

        f32 = jnp.float32
        weights = pl.pallas_call(
            functools.partial(weight_kernel, stages, block),
            out_shape=jax.ShapeDtypeStruct((pool_size, count), f32),
            in_specs=[SMEM] + [pl.BlockSpec(memory_space=pltpu.HBM)] * 4,
            out_specs=VMEM,
            scratch_shapes=[
                pltpu.VMEM(neg_ids.shape[::-1], jnp.int32),
                pltpu.VMEM(neg_ids.shape[::-1], jnp.int32),
                pltpu.VMEM((1, count), jnp.int32),
                pltpu.SemaphoreType.DMA((3,)),
            ],
            cost_estimate=cost(10000000, 200000),
            compiler_params=WIDE_LIMIT,
            name="weights",
        )(me_arr, neg_ids.T, neg_mask.T, neg_counts.reshape(1, count), queries)
        early = pool[: n // 2] + pool[n : n + n // 2]
        late = pool[n // 2 : n] + pool[n + n // 2 :]
        rawa, scalea, qs = pl.pallas_call(
            functools.partial(early_kernel, n),
            out_shape=(
                jax.ShapeDtypeStruct((half, count), f32),
                jax.ShapeDtypeStruct((half, 128), f32),
                jax.ShapeDtypeStruct((1, count), f32),
            ),
            in_specs=[VMEM] * (n + 1),
            out_specs=(VMEM,) * 3,
            cost_estimate=cost(2 * half * count * width, 2000000),
            compiler_params=LIMIT,
            name="early_scores",
        )(*early, queries)
        sent, pa, qc, loss, inner = pl.pallas_call(
            functools.partial(loss_kernel, n, stages, block),
            out_shape=(
                jax.ShapeDtypeStruct((half, width), jnp.bfloat16),
                jax.ShapeDtypeStruct((half, count), jnp.bfloat16),
                jax.ShapeDtypeStruct((pool_size, count), jnp.bfloat16),
                jax.ShapeDtypeStruct((1, count), f32),
                jax.ShapeDtypeStruct((1, count), f32),
            ),
            in_specs=[VMEM] * n + [SMEM] + [VMEM] * 7,
            out_specs=(VMEM,) * 5,
            cost_estimate=cost(4 * half * count * width, 2000000),
            compiler_params=LIMIT,
            name="loss",
        )(*late, me_arr, queries, rawa, scalea, weights, qs, pos_ids.reshape(1, count), d_loss.reshape(1, count))
        total = pl.pallas_call(
            kept_kernel,
            out_shape=jax.ShapeDtypeStruct((half, width), f32),
            in_specs=[VMEM] * 2,
            out_specs=VMEM,
            cost_estimate=cost(2 * half * count * width, 2000000),
            compiler_params=LIMIT,
            name="kept_terms",
        )(pa, queries)

        received = swap(sent, "loop", loop, stages[-1][1])
        for _, m in stages[2:-1][::-1]:
            total = total + wide(received)
            part = total.shape[0] // 2
            received = swap(total[part:].astype(jnp.bfloat16), "loop", loop, m)
            total = total[:part]
        part = total.shape[0] // 4
        kept0, kept1, sent0, sent1 = sum_call(
            split_kernel, [((part, width), f32)] * 2 + [((part, width), jnp.bfloat16)] * 2, total, received
        )
        got1 = swap(sent1, "loop", loop, stages[1][1])
        got0 = swap(sent0, "loop", loop, stages[1][1])
        term = ((block, width), jnp.bfloat16)
        far2, far3 = sum_call(far_kernel, [term, term], kept1, got1)
        got3 = swap(far3, "loop", loop, stages[0][3])
        got2 = swap(far2, "loop", loop, stages[0][2])
        total, far1 = sum_call(far_kernel, [((block, width), f32), term], kept0, got0)
        got1 = swap(far1, "loop", loop, stages[0][1])
        total = total + wide(got1) + wide(got2) + wide(got3)
        moved = []
        for b in range(narrow.bit_length() - 1):
            if moved:
                total = total + wide(moved.pop())
            moved.append(swap(total.astype(jnp.bfloat16), "narrow", narrow, 1 << b))

        step = 512
        calls = 2
        steps = width // step // calls
        grad_queries = None
        for k in range(calls):
            before = [] if grad_queries is None else [grad_queries]
            grad_queries = pl.pallas_call(
                functools.partial(query_kernel, 2 * n, k * steps),
                out_shape=jax.ShapeDtypeStruct(queries.shape, jnp.bfloat16),
                grid=(steps,),
                in_specs=[VMEM] * (2 * n + 3) + [pl.BlockSpec(memory_space=pl.ANY)] * len(before),
                out_specs=pl.BlockSpec((count, step), lambda i, k=k: (0, i + k * steps)),
                input_output_aliases={2 * n + 3: 0} if before else {},
                scratch_shapes=[pltpu.VMEM((count, pool_size), jnp.bfloat16), pltpu.VMEM((count, 128), f32)],
                cost_estimate=cost(2 * pool_size * count * width // calls, 5000000 // calls),
                compiler_params=LIMIT,
            )(*pool, qc, queries, inner, *before)
        grad_passages = pl.pallas_call(
            functools.partial(passage_kernel, len(moved)),
            out_shape=jax.ShapeDtypeStruct(passages.shape, jnp.bfloat16),
            in_specs=[VMEM] * (2 + len(moved)),
            out_specs=VMEM,
            cost_estimate=cost(1000000, 200000),
            compiler_params=LIMIT,
            name="passage_gradients",
        )(passages, total, *moved)
        return loss.reshape(count), grad_queries, grad_passages

    return local


def solution(mesh):
    return jax.shard_map(
        make_local(mesh.shape["loop"], mesh.shape["narrow"]),
        mesh=mesh,
        in_specs=(
            P(("loop", "narrow"), None),
            P("loop", None),
            P(("loop", "narrow")),
            P(("loop", "narrow"), None),
            P(("loop", "narrow"), None),
            P(("loop", "narrow")),
            P(("loop", "narrow")),
        ),
        out_specs=(P(("loop", "narrow")), P(("loop", "narrow"), None), P("loop", None)),
        check_vma=False,
    )
```

```python
import functools

import jax
import jax.numpy as jnp
from jax import lax
from jax.experimental import pallas as pl
from jax.experimental.pallas import tpu as pltpu
from jax.sharding import PartitionSpec as P


logit_scale = 50.0
norm_eps = 1e-06


LIMIT = pltpu.CompilerParams(vmem_limit_bytes=16 * 1024 * 1024)
WIDE_LIMIT = pltpu.CompilerParams(vmem_limit_bytes=56 * 1024 * 1024)
VMEM = pl.BlockSpec(memory_space=pltpu.VMEM)
SMEM = pl.BlockSpec(memory_space=pltpu.SMEM)
HBM = pl.BlockSpec(memory_space=pltpu.HBM)
F32 = jnp.float32
BF16 = jnp.bfloat16
ROWS = (((1,), (1,)), ((), ()))


def stage_masks(size):
    bits = [1 << b for b in range(size.bit_length() - 1)][::-1]
    first = [0, bits[1] | 1, bits[0] | 1, bits[0] | bits[1] | 1]
    return [first] + [[0, b | 1] for b in bits[2:]]


def swap(x, axis, size, mask):
    return lax.ppermute(x, axis, [(i, i ^ mask) for i in range(size)])


def wide(x):
    return x.astype(F32)


def call(kernel, outs, args, in_specs=None, limit=LIMIT, flops=200000, moved=1000000, **options):
    options.setdefault("out_specs", (VMEM,) * len(outs))
    return pl.pallas_call(
        kernel,
        out_shape=tuple(jax.ShapeDtypeStruct(*out) for out in outs),
        in_specs=in_specs or [VMEM] * len(args),
        cost_estimate=pl.CostEstimate(flops=flops, bytes_accessed=moved, transcendentals=0),
        compiler_params=limit,
        **options,
    )(*args)


def passage_ids(stages, block, shape, me):
    row = lax.broadcasted_iota(jnp.int32, shape, 0)
    place = row // block
    digits, owner = place, jnp.full(shape, me, jnp.int32)
    for masks in stages:
        digit = digits % len(masks)
        digits = digits // len(masks)
        chosen = jnp.zeros(shape, jnp.int32)
        for k, m in enumerate(masks[1:]):
            chosen = jnp.where(digit == k + 1, m, chosen)
        owner = owner ^ chosen
    return owner * block + (row - place * block)


def weight_kernel(stages, block, me_ref, *refs):
    sources, (w_ref, pack_ref), scratch, sems = refs[:5], refs[6:8], refs[8:13], refs[13]
    copies = [pltpu.make_async_copy(src, dst, sems.at[k]) for k, (src, dst) in enumerate(zip(sources, scratch))]
    for copy in copies:
        copy.start()
    half = w_ref.shape[0]
    mine = passage_ids(stages[:-1], block, w_ref.shape, me_ref[0])
    others = passage_ids(stages[:-1], block, w_ref.shape, me_ref[0] ^ stages[-1][1])
    for copy in copies:
        copy.wait()
    ids_ref, mask_ref, count_ref, pos_ref, dl_ref = scratch
    slot = lax.broadcasted_iota(jnp.int32, ids_ref.shape, 0)
    named = jnp.where((mask_ref[...] == 1) & (slot < count_ref[...]), ids_ref[...], -1)
    w_mine = jnp.ones(w_ref.shape, F32)
    w_others = jnp.ones(w_ref.shape, F32)
    for k in range(ids_ref.shape[0]):
        w_mine = w_mine + jnp.where(named[k : k + 1] == mine, 1.0, 0.0)
        w_others = w_others + jnp.where(named[k : k + 1] == others, 1.0, 0.0)
    w_ref[...] = w_mine
    pack_ref[:half] = w_others
    pack_ref[half : half + 1] = dl_ref[...]
    pack_ref[half + 1 : half + 2] = pos_ref[...].astype(F32)
    pack_ref[half + 2 :] = jnp.zeros((6, w_ref.shape[1]), F32)


def raw_and_scale(refs, queries):
    rows = jnp.concatenate([r[...] for r in refs], axis=0)
    f = wide(rows)
    scale = lax.rsqrt(jnp.sum(f * f, axis=1, keepdims=True) + norm_eps)
    raw = [lax.dot_general(rows, q, ROWS, preferred_element_type=F32) for q in queries]
    return rows, jnp.concatenate(raw, axis=1), scale


def early_kernel(n, *refs):
    q_ref, other_ref, raw_ref, scale_ref, qs_ref = refs[n:]
    queries = [q_ref[...], other_ref[...]]
    _, raw, scale = raw_and_scale(refs[:n], queries)
    raw_ref[...] = raw
    scale_ref[...] = jnp.broadcast_to(scale, scale_ref.shape)
    for k, q in enumerate(queries):
        f = wide(q)
        own = lax.rsqrt(jnp.sum(f * f, axis=1, keepdims=True) + norm_eps)
        qs_ref[:, k * q.shape[0] : (k + 1) * q.shape[0]] = jnp.broadcast_to(own, (own.shape[0], 128)).T[:1]


def late_kernel(n, stages, block, me_ref, *refs):
    early, late = refs[: n // 2], refs[n // 2 : n]
    q_ref, other_ref, raw_ref, scale_ref, qs_ref, w_ref, pack_ref, pos_ref = refs[n : n + 8]
    pool_ref, all_ref, scales_ref, terms_ref, chosen_ref, sums_ref = refs[n + 8 :]
    half = w_ref.shape[0]
    rows, raw, scale = raw_and_scale(late, [q_ref[...], other_ref[...]])
    raw = jnp.concatenate([raw_ref[...], raw], axis=0)
    scale = jnp.concatenate([scale_ref[...], jnp.broadcast_to(scale, (scale.shape[0], 128))], axis=0)
    scores = logit_scale * (raw * scale[:, :1] * qs_ref[...])
    terms = jnp.concatenate([w_ref[...], pack_ref[:half]], axis=1) * jnp.exp(scores)
    positive = jnp.concatenate([pos_ref[...], pack_ref[half + 1 : half + 2].astype(jnp.int32)], axis=1)
    chosen = passage_ids(stages[:-1], block, scores.shape, me_ref[0]) == positive
    sums_ref[:1] = jnp.sum(terms, axis=0, keepdims=True)
    sums_ref[1:2] = jnp.sum(jnp.where(chosen, scores, 0.0), axis=0, keepdims=True)
    sums_ref[2:] = jnp.zeros((6, scores.shape[1]), F32)
    terms_ref[...] = terms
    chosen_ref[...] = jnp.where(chosen, 1.0, 0.0)
    all_ref[...] = raw
    scales_ref[...] = scale
    part = half - rows.shape[0]
    pool_ref[:part] = jnp.concatenate([r[...] for r in early], axis=0)
    pool_ref[part:] = rows


def coef_kernel(*refs):
    q_ref, other_ref, raw_ref, scale_ref, qs_ref, terms_ref, chosen_ref, sums_ref, got_ref, dl_ref, pack_ref = refs[:11]
    kept_ref, sent_ref, qc_ref, share_ref, loss_ref, inner_ref = refs[11:]
    count = q_ref.shape[0]
    half = raw_ref.shape[0]
    sums = sums_ref[...] + jnp.concatenate([got_ref[:, count:], got_ref[:, :count]], axis=1)
    dl = jnp.concatenate([dl_ref[...], pack_ref[half : half + 1]], axis=1)
    coef = (logit_scale * dl) * (terms_ref[...] / sums[:1] - chosen_ref[...])
    pcoef = coef * qs_ref[...]
    pc = pcoef.astype(BF16)
    total = jnp.dot(pc[:, :count], q_ref[...], preferred_element_type=F32)
    total = total + jnp.dot(pc[:, count:], other_ref[...], preferred_element_type=F32)
    part = kept_ref.shape[0]
    kept_ref[...] = total[:part]
    sent_ref[...] = total[part:].astype(BF16)
    qc = wide((pcoef * scale_ref[:, :1]).astype(BF16))
    inner = jnp.sum(qc * raw_ref[...], axis=0, keepdims=True)
    qc_ref[...] = qc[:, :count].astype(BF16)
    share_ref[:half] = qc[:, count:]
    share_ref[half : half + 1] = inner[:, count:]
    share_ref[half + 1 :] = jnp.zeros((7, count), F32)
    inner_ref[...] = inner[:, :count]
    loss_ref[...] = jnp.log(sums[:1, :count]) - sums[1:2, :count]


def query_kernel(first, *refs):
    pool_ref, others_ref, qc_ref, share_ref, inner_ref, qs_ref, q_ref = refs[:7]
    out_ref, coef_ref, column_ref = refs[-3:]
    step = out_ref.shape[1]
    count = q_ref.shape[0]
    half = qc_ref.shape[0]

    @pl.when(pl.program_id(0) == 0)
    def _():
        coef_ref[:, :half] = qc_ref[...].T
        coef_ref[:, half:] = share_ref[:half].astype(BF16).T
        qs = qs_ref[:, :count]
        inner = (inner_ref[...] + share_ref[half : half + 1]) * qs * qs
        column_ref[...] = jnp.broadcast_to(inner, (128, count)).T

    at = pl.ds(pl.multiple_of((first + pl.program_id(0)) * step, step), step)
    rows = jnp.concatenate([pool_ref[:, at], others_ref[:, at]], axis=0)
    qdir = jnp.dot(coef_ref[...], rows, preferred_element_type=F32)
    out_ref[...] = (qdir - wide(q_ref[:, at]) * column_ref[:, :1]).astype(BF16)


def far_kernel(kept_ref, got_ref, *out_refs):
    total = kept_ref[...] + wide(got_ref[...])
    part = out_refs[0].shape[0]
    for k, ref in enumerate(out_refs):
        ref[...] = total[k * part : (k + 1) * part].astype(ref.dtype)


def passage_kernel(n, p_ref, total_ref, *refs):
    out_ref = refs[n]
    pdir = total_ref[...]
    for r in refs[:n]:
        pdir = pdir + wide(r[...])
    f = wide(p_ref[...])
    scale = lax.rsqrt(jnp.sum(f * f, axis=1, keepdims=True) + norm_eps)
    unit = f * scale
    inner = jnp.sum(unit * pdir, axis=1, keepdims=True)
    out_ref[...] = (scale * (pdir - unit * inner)).astype(BF16)


def make_local(loop, narrow):
    stages = stage_masks(loop)

    def body(queries, passages, pos_ids, neg_ids, neg_mask, neg_counts, d_loss):
        me = lax.axis_index("loop").astype(jnp.int32).reshape(1)
        block, width = passages.shape
        count, slots = neg_ids.shape
        half = loop * block // 2
        core = stages[-1][1]

        def cross(x, mask):
            return swap(x, "loop", loop, mask)

        first = [passages] + [cross(passages, m) for m in stages[0][1:]]
        pool = [jnp.concatenate(first[k : k + 2], axis=0) for k in (0, 2)]
        for _, m in stages[1:-2]:
            pool = [jnp.concatenate(pool + [cross(t, m) for t in pool], axis=0)]
        pool = pool + [cross(t, stages[-2][1]) for t in pool]
        n = len(pool)

        others = cross(queries, core)
        row = lambda x: x.reshape(1, count)
        weights, pack = call(
            functools.partial(weight_kernel, stages, block),
            [((half, count), F32), ((half + 8, count), F32)],
            (me, neg_ids.T, neg_mask.T, row(neg_counts), row(pos_ids), row(d_loss), queries),
            in_specs=[SMEM] + [HBM] * 6,
            limit=WIDE_LIMIT,
            flops=10000000,
            scratch_shapes=[pltpu.VMEM((slots, count), jnp.int32)] * 2
            + [pltpu.VMEM((1, count), jnp.int32)] * 2
            + [pltpu.VMEM((1, count), F32), pltpu.SemaphoreType.DMA((5,))],
        )
        pack = cross(pack, core)

        both = 2 * count
        raw, scale, qs = call(
            functools.partial(early_kernel, n // 2),
            [((half // 2, both), F32), ((half // 2, 128), F32), ((1, both), F32)],
            (*pool[: n // 2], queries, others),
            flops=2 * half * count * width,
        )
        rows, raw, scale, terms, chosen, sums = call(
            functools.partial(late_kernel, n, stages, block),
            [((half, width), BF16), ((half, both), F32), ((half, 128), F32)] + [((half, both), F32)] * 2 + [((8, both), F32)],
            (me, *pool, queries, others, raw, scale, qs, weights, pack, row(pos_ids)),
            in_specs=[SMEM] + [VMEM] * (n + 8),
            flops=2 * half * count * width,
        )
        kept, sent, qc, share, loss, inner = call(
            coef_kernel,
            [((half // 2, width), F32), ((half // 2, width), BF16), ((half, count), BF16), ((half + 8, count), F32)]
            + [((1, count), F32)] * 2,
            (queries, others, raw, scale, qs, terms, chosen, sums, cross(sums, core), row(d_loss), pack),
            flops=4 * half * count * width,
        )

        got = cross(sent, stages[-2][1])
        for _, m in stages[1:-2][::-1]:
            total = kept + wide(got)
            part = total.shape[0] // 2
            kept, got = total[:part], cross(total[part:].astype(BF16), m)
        term = (block, width)
        total, *terms = call(far_kernel, [(term, F32)] + [(term, BF16)] * 3, (kept, got))
        moved = [cross(terms[k - 1], stages[0][k]) for k in (3, 2, 1)]
        for t in moved:
            total = total + wide(t)
        moved = []
        for b in range(narrow.bit_length() - 1):
            if moved:
                total = total + wide(moved.pop())
            moved.append(swap(total.astype(BF16), "narrow", narrow, 1 << b))

        step = 512
        calls = 2
        steps = width // step // calls
        grad_queries = []
        operands = (rows, cross(rows, core), qc, cross(share, core), inner, qs, queries)
        for k in range(calls):
            grad_queries = call(
                functools.partial(query_kernel, k * steps),
                [(queries.shape, BF16)],
                (*operands, *grad_queries),
                grid=(steps,),
                in_specs=[VMEM] * 7 + [pl.BlockSpec(memory_space=pl.ANY)] * len(grad_queries),
                out_specs=(pl.BlockSpec((count, step), lambda i, k=k: (0, i + k * steps)),),
                input_output_aliases={7: 0} if grad_queries else {},
                scratch_shapes=[pltpu.VMEM((count, 2 * half), BF16), pltpu.VMEM((count, 128), F32)],
                flops=4 * half * count * width // calls,
                moved=3000000,
            )
        (grad_passages,) = call(
            functools.partial(passage_kernel, len(moved)), [(passages.shape, BF16)], (passages, total, *moved)
        )
        return loss.reshape(count), *grad_queries, grad_passages

    return body


def solution(mesh):
    both = ("loop", "narrow")
    return jax.shard_map(
        make_local(mesh.shape["loop"], mesh.shape["narrow"]),
        mesh=mesh,
        in_specs=(P(both, None), P("loop", None), P(both), P(both, None), P(both, None), P(both), P(both)),
        out_specs=(P(both), P(both, None), P("loop", None)),
        check_vma=False,
    )
```

```python
import functools

import jax
import jax.numpy as jnp
from jax import lax
from jax.experimental import pallas as pl
from jax.experimental.pallas import tpu as pltpu
from jax.sharding import PartitionSpec as P


logit_scale = 50.0
norm_eps = 1e-06


LIMIT = pltpu.CompilerParams(vmem_limit_bytes=16 * 1024 * 1024)
WIDE_LIMIT = pltpu.CompilerParams(vmem_limit_bytes=56 * 1024 * 1024)
VMEM = pl.BlockSpec(memory_space=pltpu.VMEM)
SMEM = pl.BlockSpec(memory_space=pltpu.SMEM)
HBM = pl.BlockSpec(memory_space=pltpu.HBM)
F32 = jnp.float32
BF16 = jnp.bfloat16
ROWS = (((1,), (1,)), ((), ()))


def stage_masks(size):
    bits = [1 << b for b in range(size.bit_length() - 1)][::-1]
    first = [0, bits[1] | 1, bits[0] | 1, bits[0] | bits[1] | 1]
    return [first] + [[0, b | 1] for b in bits[2:]]


def swap(x, axis, size, mask):
    return lax.ppermute(x, axis, [(i, i ^ mask) for i in range(size)])


def wide(x):
    return x.astype(F32)


def call(kernel, outs, args, in_specs=None, limit=LIMIT, flops=200000, moved=1000000, **options):
    options.setdefault("out_specs", (VMEM,) * len(outs))
    return pl.pallas_call(
        kernel,
        out_shape=tuple(jax.ShapeDtypeStruct(*out) for out in outs),
        in_specs=in_specs or [VMEM] * len(args),
        cost_estimate=pl.CostEstimate(flops=flops, bytes_accessed=moved, transcendentals=0),
        compiler_params=limit,
        **options,
    )(*args)


def split_index(x, n):
    if n & (n - 1):
        return x // n, x % n
    return x >> (n.bit_length() - 1), x & (n - 1)


def passage_ids(stages, block, shape, me):
    row = lax.broadcasted_iota(jnp.int32, shape, 0)
    digits, inside = split_index(row, block)
    owner = jnp.full(shape, me, jnp.int32)
    for masks in stages:
        digits, digit = split_index(digits, len(masks))
        chosen = jnp.zeros(shape, jnp.int32)
        for k, m in enumerate(masks[1:]):
            chosen = jnp.where(digit == k + 1, m, chosen)
        owner = owner ^ chosen
    return owner * block + inside


def weight_kernel(stages, block, me_ref, *refs):
    sources, (w_ref, pack_ref), scratch, sems = refs[:5], refs[6:8], refs[8:13], refs[13]
    copies = [pltpu.make_async_copy(src, dst, sems.at[k]) for k, (src, dst) in enumerate(zip(sources, scratch))]
    for copy in copies:
        copy.start()
    half = w_ref.shape[0]
    mine = passage_ids(stages[:-1], block, w_ref.shape, me_ref[0])
    others = passage_ids(stages[:-1], block, w_ref.shape, me_ref[0] ^ stages[-1][1])
    for copy in copies:
        copy.wait()
    ids_ref, mask_ref, count_ref, pos_ref, dl_ref = scratch
    slot = lax.broadcasted_iota(jnp.int32, ids_ref.shape, 0)
    named = jnp.where((mask_ref[...] == 1) & (slot < count_ref[...]), ids_ref[...], -1)
    w_mine = jnp.ones(w_ref.shape, F32)
    w_others = jnp.ones(w_ref.shape, F32)
    for k in range(ids_ref.shape[0]):
        w_mine = w_mine + jnp.where(named[k : k + 1] == mine, 1.0, 0.0)
        w_others = w_others + jnp.where(named[k : k + 1] == others, 1.0, 0.0)
    w_ref[...] = w_mine
    pack_ref[:half] = w_others
    pack_ref[half : half + 1] = dl_ref[...]
    pack_ref[half + 1 : half + 2] = pos_ref[...].astype(F32)
    pack_ref[half + 2 :] = jnp.zeros((6, w_ref.shape[1]), F32)


def raw_and_scale(refs, queries):
    rows = jnp.concatenate([r[...] for r in refs], axis=0)
    f = wide(rows)
    scale = lax.rsqrt(jnp.sum(f * f, axis=1, keepdims=True) + norm_eps)
    raw = [lax.dot_general(rows, q, ROWS, preferred_element_type=F32) for q in queries]
    return rows, jnp.concatenate(raw, axis=1), scale


def early_kernel(n, *refs):
    q_ref, other_ref, raw_ref, scale_ref, qs_ref = refs[n:]
    queries = [q_ref[...], other_ref[...]]
    _, raw, scale = raw_and_scale(refs[:n], queries)
    raw_ref[...] = raw
    scale_ref[...] = jnp.broadcast_to(scale, scale_ref.shape)
    for k, q in enumerate(queries):
        f = wide(q)
        own = lax.rsqrt(jnp.sum(f * f, axis=1, keepdims=True) + norm_eps)
        qs_ref[:, k * q.shape[0] : (k + 1) * q.shape[0]] = jnp.broadcast_to(own, (own.shape[0], 128)).T[:1]


def late_kernel(n, stages, block, me_ref, *refs):
    early, late = refs[: n // 2], refs[n // 2 : n]
    q_ref, other_ref, raw_ref, scale_ref, qs_ref, w_ref, pack_ref, pos_ref = refs[n : n + 8]
    pool_ref, all_ref, scales_ref, terms_ref, chosen_ref, sums_ref = refs[n + 8 :]
    half = w_ref.shape[0]
    rows, raw, scale = raw_and_scale(late, [q_ref[...], other_ref[...]])
    raw = jnp.concatenate([raw_ref[...], raw], axis=0)
    scale = jnp.concatenate([scale_ref[...], jnp.broadcast_to(scale, (scale.shape[0], 128))], axis=0)
    scores = logit_scale * (raw * scale[:, :1] * qs_ref[...])
    terms = jnp.concatenate([w_ref[...], pack_ref[:half]], axis=1) * jnp.exp(scores)
    positive = jnp.concatenate([pos_ref[...], pack_ref[half + 1 : half + 2].astype(jnp.int32)], axis=1)
    chosen = passage_ids(stages[:-1], block, scores.shape, me_ref[0]) == positive
    sums_ref[:1] = jnp.sum(terms, axis=0, keepdims=True)
    sums_ref[1:2] = jnp.sum(jnp.where(chosen, scores, 0.0), axis=0, keepdims=True)
    sums_ref[2:] = jnp.zeros((6, scores.shape[1]), F32)
    terms_ref[...] = terms
    chosen_ref[...] = jnp.where(chosen, 1.0, 0.0)
    all_ref[...] = raw
    scales_ref[...] = scale
    part = half - rows.shape[0]
    pool_ref[:part] = jnp.concatenate([r[...] for r in early], axis=0)
    pool_ref[part:] = rows


def direction_terms(pcoef, columns, q_ref, other_ref, kept_ref, sent_ref):
    count = q_ref.shape[0]
    pc = pcoef.astype(BF16)
    total = jnp.dot(pc[:, :count], q_ref[:, columns], preferred_element_type=F32)
    total = total + jnp.dot(pc[:, count:], other_ref[:, columns], preferred_element_type=F32)
    part = kept_ref.shape[0]
    kept_ref[...] = total[:part]
    sent_ref[...] = total[part:].astype(BF16)


def coef_kernel(*refs):
    q_ref, other_ref, qs_ref, terms_ref, chosen_ref, sums_ref, got_ref, dl_ref, pack_ref = refs[:9]
    kept_ref, sent_ref, coef_ref, all_ref = refs[9:]
    count = q_ref.shape[0]
    half = terms_ref.shape[0]
    sums = sums_ref[...] + jnp.concatenate([got_ref[:, count:], got_ref[:, :count]], axis=1)
    dl = jnp.concatenate([dl_ref[...], pack_ref[half : half + 1]], axis=1)
    coef = (logit_scale * dl) * (terms_ref[...] / sums[:1] - chosen_ref[...])
    pcoef = coef * qs_ref[...]
    direction_terms(pcoef, slice(0, kept_ref.shape[1]), q_ref, other_ref, kept_ref, sent_ref)
    coef_ref[...] = pcoef
    all_ref[...] = sums


def other_columns_kernel(q_ref, other_ref, coef_ref, kept_ref, sent_ref):
    width = q_ref.shape[1]
    direction_terms(coef_ref[...], slice(width - kept_ref.shape[1], width), q_ref, other_ref, kept_ref, sent_ref)


def share_kernel(raw_ref, scale_ref, coef_ref, sums_ref, qc_ref, share_ref, loss_ref, inner_ref):
    half = raw_ref.shape[0]
    count = qc_ref.shape[1]
    qc = wide((coef_ref[...] * scale_ref[:, :1]).astype(BF16))
    inner = jnp.sum(qc * raw_ref[...], axis=0, keepdims=True)
    qc_ref[...] = qc[:, :count].astype(BF16)
    share_ref[:half] = qc[:, count:]
    share_ref[half : half + 1] = inner[:, count:]
    share_ref[half + 1 :] = jnp.zeros((7, count), F32)
    inner_ref[...] = inner[:, :count]
    loss_ref[...] = jnp.log(sums_ref[:1, :count]) - sums_ref[1:2, :count]


def query_kernel(first, *refs):
    pool_ref, others_ref, qc_ref, share_ref, inner_ref, qs_ref, q_ref = refs[:7]
    out_ref, coef_ref, column_ref = refs[-3:]
    step = out_ref.shape[1]
    count = q_ref.shape[0]
    half = qc_ref.shape[0]

    @pl.when(pl.program_id(0) == 0)
    def _():
        coef_ref[:, :half] = qc_ref[...].T
        coef_ref[:, half:] = share_ref[:half].astype(BF16).T
        qs = qs_ref[:, :count]
        inner = (inner_ref[...] + share_ref[half : half + 1]) * qs * qs
        column_ref[...] = jnp.broadcast_to(inner, (128, count)).T

    at = pl.ds(pl.multiple_of((first + pl.program_id(0)) * step, step), step)
    rows = jnp.concatenate([pool_ref[:, at], others_ref[:, at]], axis=0)
    qdir = jnp.dot(coef_ref[...], rows, preferred_element_type=F32)
    out_ref[...] = (qdir - wide(q_ref[:, at]) * column_ref[:, :1]).astype(BF16)


def far_kernel(n, *refs):
    at = 0
    for kept_ref, got_ref in zip(refs[:n], refs[n : 2 * n]):
        total = kept_ref[...] + wide(got_ref[...])
        columns = slice(at, at + total.shape[1])
        at += total.shape[1]
        part = refs[2 * n].shape[0]
        for k, ref in enumerate(refs[2 * n :]):
            ref[:, columns] = total[k * part : (k + 1) * part].astype(ref.dtype)


def passage_kernel(n, p_ref, total_ref, *refs):
    out_ref = refs[n]
    pdir = total_ref[...]
    for r in refs[:n]:
        pdir = pdir + wide(r[...])
    f = wide(p_ref[...])
    scale = lax.rsqrt(jnp.sum(f * f, axis=1, keepdims=True) + norm_eps)
    unit = f * scale
    inner = jnp.sum(unit * pdir, axis=1, keepdims=True)
    out_ref[...] = (scale * (pdir - unit * inner)).astype(BF16)


def make_local(loop, narrow):
    stages = stage_masks(loop)

    def body(queries, passages, pos_ids, neg_ids, neg_mask, neg_counts, d_loss):
        me = lax.axis_index("loop").astype(jnp.int32).reshape(1)
        block, width = passages.shape
        count, slots = neg_ids.shape
        half = loop * block // 2
        core = stages[-1][1]

        def cross(x, mask):
            return swap(x, "loop", loop, mask)

        first = [passages] + [cross(passages, m) for m in stages[0][1:]]
        pool = [jnp.concatenate(first[k : k + 2], axis=0) for k in (0, 2)]
        for _, m in stages[1:-2]:
            pool = [jnp.concatenate(pool + [cross(t, m) for t in pool], axis=0)]
        pool = pool + [cross(t, stages[-2][1]) for t in pool]
        n = len(pool)

        others = cross(queries, core)
        row = lambda x: x.reshape(1, count)
        weights, pack = call(
            functools.partial(weight_kernel, stages, block),
            [((half, count), F32), ((half + 8, count), F32)],
            (me, neg_ids.T, neg_mask.T, row(neg_counts), row(pos_ids), row(d_loss), queries),
            in_specs=[SMEM] + [HBM] * 6,
            limit=WIDE_LIMIT,
            flops=10000000,
            scratch_shapes=[pltpu.VMEM((slots, count), jnp.int32)] * 2
            + [pltpu.VMEM((1, count), jnp.int32)] * 2
            + [pltpu.VMEM((1, count), F32), pltpu.SemaphoreType.DMA((5,))],
        )
        pack = cross(pack, core)

        both = 2 * count
        raw, scale, qs = call(
            functools.partial(early_kernel, n // 2),
            [((half // 2, both), F32), ((half // 2, 128), F32), ((1, both), F32)],
            (*pool[: n // 2], queries, others),
            flops=2 * half * count * width,
        )
        rows, raw, scale, terms, chosen, sums = call(
            functools.partial(late_kernel, n, stages, block),
            [((half, width), BF16), ((half, both), F32), ((half, 128), F32)] + [((half, both), F32)] * 2 + [((8, both), F32)],
            (me, *pool, queries, others, raw, scale, qs, weights, pack, row(pos_ids)),
            in_specs=[SMEM] + [VMEM] * (n + 8),
            flops=2 * half * count * width,
        )
        piece = (half // 2, width // 2)
        kept0, sent0, coef, sums = call(
            coef_kernel,
            [(piece, F32), (piece, BF16), ((half, both), F32), ((8, both), F32)],
            (queries, others, qs, terms, chosen, sums, cross(sums, core), row(d_loss), pack),
            flops=2 * half * count * width,
        )
        near = stages[-2][1]
        got0 = cross(sent0, near)
        kept1, sent1 = call(
            other_columns_kernel, [(piece, F32), (piece, BF16)], (queries, others, coef), flops=2 * half * count * width
        )
        qc, share, loss, inner = call(
            share_kernel,
            [((half, count), BF16), ((half + 8, count), F32)] + [((1, count), F32)] * 2,
            (raw, scale, coef, sums),
        )

        kept, got = [kept0, kept1], [got0, cross(sent1, near)]
        for _, m in stages[1:-2][::-1]:
            total = jnp.concatenate(kept, axis=1) + wide(jnp.concatenate(got, axis=1))
            part = total.shape[0] // 2
            kept, got = [total[:part]], [cross(total[part:].astype(BF16), m)]
        term = (block, width)
        total, *terms = call(
            functools.partial(far_kernel, len(kept)), [(term, F32)] + [(term, BF16)] * 3, (*kept, *got)
        )
        moved = [cross(terms[k - 1], stages[0][k]) for k in (3, 2, 1)]
        for t in moved:
            total = total + wide(t)
        moved = []
        for b in range(narrow.bit_length() - 1):
            if moved:
                total = total + wide(moved.pop())
            moved.append(swap(total.astype(BF16), "narrow", narrow, 1 << b))

        step = 512
        calls = 2
        steps = width // step // calls
        grad_queries = []
        operands = (rows, cross(rows, core), qc, cross(share, core), inner, qs, queries)
        for k in range(calls):
            grad_queries = call(
                functools.partial(query_kernel, k * steps),
                [(queries.shape, BF16)],
                (*operands, *grad_queries),
                grid=(steps,),
                in_specs=[VMEM] * 7 + [pl.BlockSpec(memory_space=pl.ANY)] * len(grad_queries),
                out_specs=(pl.BlockSpec((count, step), lambda i, k=k: (0, i + k * steps)),),
                input_output_aliases={7: 0} if grad_queries else {},
                scratch_shapes=[pltpu.VMEM((count, 2 * half), BF16), pltpu.VMEM((count, 128), F32)],
                flops=4 * half * count * width // calls,
                moved=3000000,
            )
        (grad_passages,) = call(
            functools.partial(passage_kernel, len(moved)), [(passages.shape, BF16)], (passages, total, *moved)
        )
        return loss.reshape(count), *grad_queries, grad_passages

    return body


def solution(mesh):
    both = ("loop", "narrow")
    return jax.shard_map(
        make_local(mesh.shape["loop"], mesh.shape["narrow"]),
        mesh=mesh,
        in_specs=(P(both, None), P("loop", None), P(both), P(both, None), P(both, None), P(both), P(both)),
        out_specs=(P(both), P(both, None), P("loop", None)),
        check_vma=False,
    )
```

```python
import functools

import jax
import jax.numpy as jnp
from jax import lax
from jax.experimental import pallas as pl
from jax.experimental.pallas import tpu as pltpu
from jax.sharding import PartitionSpec as P


logit_scale = 50.0
norm_eps = 1e-06


LIMIT = pltpu.CompilerParams(vmem_limit_bytes=16 * 1024 * 1024)
WIDE_LIMIT = pltpu.CompilerParams(vmem_limit_bytes=56 * 1024 * 1024)
VMEM = pl.BlockSpec(memory_space=pltpu.VMEM)
SMEM = pl.BlockSpec(memory_space=pltpu.SMEM)
HBM = pl.BlockSpec(memory_space=pltpu.HBM)
F32 = jnp.float32
BF16 = jnp.bfloat16
ROWS = (((1,), (1,)), ((), ()))


def stage_masks(size):
    bits = [1 << b for b in range(size.bit_length() - 1)][::-1]
    first = [0, bits[1] | 1, bits[0] | 1, bits[0] | bits[1] | 1]
    return [first] + [[0, b | 1] for b in bits[2:]]


def swap(x, axis, size, mask):
    return lax.ppermute(x, axis, [(i, i ^ mask) for i in range(size)])


def wide(x):
    return x.astype(F32)


def call(kernel, outs, args, in_specs=None, limit=LIMIT, flops=200000, moved=1000000, **options):
    options.setdefault("out_specs", (VMEM,) * len(outs))
    return pl.pallas_call(
        kernel,
        out_shape=tuple(jax.ShapeDtypeStruct(*out) for out in outs),
        in_specs=in_specs or [VMEM] * len(args),
        cost_estimate=pl.CostEstimate(flops=flops, bytes_accessed=moved, transcendentals=0),
        compiler_params=limit,
        **options,
    )(*args)


def split_index(x, n):
    if n & (n - 1):
        return x // n, x % n
    return x >> (n.bit_length() - 1), x & (n - 1)


def passage_ids(stages, block, shape, me):
    row = lax.broadcasted_iota(jnp.int32, shape, 0)
    digits, inside = split_index(row, block)
    owner = jnp.full(shape, me, jnp.int32)
    for masks in stages:
        digits, digit = split_index(digits, len(masks))
        chosen = jnp.zeros(shape, jnp.int32)
        for k, m in enumerate(masks[1:]):
            chosen = jnp.where(digit == k + 1, m, chosen)
        owner = owner ^ chosen
    return owner * block + inside


def weight_kernel(stages, block, me_ref, *refs):
    sources, (w_ref, pack_ref), scratch, sems = refs[:5], refs[6:8], refs[8:13], refs[13]
    copies = [pltpu.make_async_copy(src, dst, sems.at[k]) for k, (src, dst) in enumerate(zip(sources, scratch))]
    for copy in copies:
        copy.start()
    half = w_ref.shape[0]
    mine = passage_ids(stages[:-1], block, w_ref.shape, me_ref[0])
    others = passage_ids(stages[:-1], block, w_ref.shape, me_ref[0] ^ stages[-1][1])
    for copy in copies:
        copy.wait()
    ids_ref, mask_ref, count_ref, pos_ref, dl_ref = scratch
    slot = lax.broadcasted_iota(jnp.int32, ids_ref.shape, 0)
    named = jnp.where((mask_ref[...] == 1) & (slot < count_ref[...]), ids_ref[...], -1)
    w_mine = jnp.ones(w_ref.shape, F32)
    w_others = jnp.ones(w_ref.shape, F32)
    for k in range(ids_ref.shape[0]):
        w_mine = w_mine + jnp.where(named[k : k + 1] == mine, 1.0, 0.0)
        w_others = w_others + jnp.where(named[k : k + 1] == others, 1.0, 0.0)
    w_ref[...] = w_mine
    pack_ref[:half] = w_others
    pack_ref[half : half + 1] = dl_ref[...]
    pack_ref[half + 1 : half + 2] = pos_ref[...].astype(F32)
    pack_ref[half + 2 :] = jnp.zeros((6, w_ref.shape[1]), F32)


def raw_and_scale(refs, queries):
    rows = jnp.concatenate([r[...] for r in refs], axis=0)
    f = wide(rows)
    scale = lax.rsqrt(jnp.sum(f * f, axis=1, keepdims=True) + norm_eps)
    raw = [lax.dot_general(rows, q, ROWS, preferred_element_type=F32) for q in queries]
    return rows, jnp.concatenate(raw, axis=1), scale


def early_kernel(n, *refs):
    q_ref, other_ref, raw_ref, scale_ref, qs_ref = refs[n:]
    queries = [q_ref[...], other_ref[...]]
    _, raw, scale = raw_and_scale(refs[:n], queries)
    raw_ref[...] = raw
    scale_ref[...] = jnp.broadcast_to(scale, scale_ref.shape)
    for k, q in enumerate(queries):
        f = wide(q)
        own = lax.rsqrt(jnp.sum(f * f, axis=1, keepdims=True) + norm_eps)
        qs_ref[:, k * q.shape[0] : (k + 1) * q.shape[0]] = jnp.broadcast_to(own, (own.shape[0], 128)).T[:1]


def late_kernel(n, stages, block, me_ref, *refs):
    early, late = refs[: n // 2], refs[n // 2 : n]
    q_ref, other_ref, raw_ref, scale_ref, qs_ref, w_ref, pack_ref, pos_ref = refs[n : n + 8]
    pool_ref, all_ref, scales_ref, terms_ref, chosen_ref, sums_ref = refs[n + 8 :]
    half = w_ref.shape[0]
    rows, raw, scale = raw_and_scale(late, [q_ref[...], other_ref[...]])
    raw = jnp.concatenate([raw_ref[...], raw], axis=0)
    scale = jnp.concatenate([scale_ref[...], jnp.broadcast_to(scale, (scale.shape[0], 128))], axis=0)
    scores = logit_scale * (raw * scale[:, :1] * qs_ref[...])
    terms = jnp.concatenate([w_ref[...], pack_ref[:half]], axis=1) * jnp.exp(scores)
    positive = jnp.concatenate([pos_ref[...], pack_ref[half + 1 : half + 2].astype(jnp.int32)], axis=1)
    chosen = passage_ids(stages[:-1], block, scores.shape, me_ref[0]) == positive
    sums_ref[:1] = jnp.sum(terms, axis=0, keepdims=True)
    sums_ref[1:2] = jnp.sum(jnp.where(chosen, scores, 0.0), axis=0, keepdims=True)
    sums_ref[2:] = jnp.zeros((6, scores.shape[1]), F32)
    terms_ref[...] = terms
    chosen_ref[...] = jnp.where(chosen, 1.0, 0.0)
    all_ref[...] = raw
    scales_ref[...] = scale
    part = half - rows.shape[0]
    pool_ref[:part] = jnp.concatenate([r[...] for r in early], axis=0)
    pool_ref[part:] = rows


def direction_terms(pcoef, columns, q_ref, other_ref, kept_ref, sent_ref):
    count = q_ref.shape[0]
    pc = pcoef.astype(BF16)
    total = jnp.dot(pc[:, :count], q_ref[:, columns], preferred_element_type=F32)
    total = total + jnp.dot(pc[:, count:], other_ref[:, columns], preferred_element_type=F32)
    part = kept_ref.shape[0]
    kept_ref[...] = total[:part]
    sent_ref[...] = total[part:].astype(BF16)


def coef_kernel(*refs):
    q_ref, other_ref, qs_ref, terms_ref, chosen_ref, sums_ref, got_ref, dl_ref, pack_ref = refs[:9]
    kept_ref, sent_ref, coef_ref, all_ref = refs[9:]
    count = q_ref.shape[0]
    half = terms_ref.shape[0]
    sums = sums_ref[...] + jnp.concatenate([got_ref[:, count:], got_ref[:, :count]], axis=1)
    dl = jnp.concatenate([dl_ref[...], pack_ref[half : half + 1]], axis=1)
    coef = (logit_scale * dl) * (terms_ref[...] / sums[:1] - chosen_ref[...])
    pcoef = coef * qs_ref[...]
    direction_terms(pcoef, slice(0, kept_ref.shape[1]), q_ref, other_ref, kept_ref, sent_ref)
    coef_ref[...] = pcoef
    all_ref[...] = sums


def other_columns_kernel(q_ref, other_ref, coef_ref, kept_ref, sent_ref):
    width = q_ref.shape[1]
    direction_terms(coef_ref[...], slice(width - kept_ref.shape[1], width), q_ref, other_ref, kept_ref, sent_ref)


def share_kernel(raw_ref, scale_ref, coef_ref, sums_ref, qc_ref, share_ref, loss_ref, inner_ref):
    half = raw_ref.shape[0]
    count = qc_ref.shape[1]
    qc = wide((coef_ref[...] * scale_ref[:, :1]).astype(BF16))
    inner = jnp.sum(qc * raw_ref[...], axis=0, keepdims=True)
    qc_ref[...] = qc[:, :count].astype(BF16)
    share_ref[:half] = qc[:, count:]
    share_ref[half : half + 1] = inner[:, count:]
    share_ref[half + 1 :] = jnp.zeros((7, count), F32)
    inner_ref[...] = inner[:, :count]
    loss_ref[...] = jnp.log(sums_ref[:1, :count]) - sums_ref[1:2, :count]


def query_kernel(first, *refs):
    pool_ref, others_ref, qc_ref, share_ref, inner_ref, qs_ref, q_ref = refs[:7]
    out_ref, coef_ref, column_ref = refs[-3:]
    step = out_ref.shape[1]
    count = q_ref.shape[0]
    half = qc_ref.shape[0]

    @pl.when(pl.program_id(0) == 0)
    def _():
        coef_ref[:, :half] = qc_ref[...].T
        coef_ref[:, half:] = share_ref[:half].astype(BF16).T
        qs = qs_ref[:, :count]
        inner = (inner_ref[...] + share_ref[half : half + 1]) * qs * qs
        column_ref[...] = jnp.broadcast_to(inner, (128, count)).T

    at = pl.ds(pl.multiple_of((first + pl.program_id(0)) * step, step), step)
    rows = jnp.concatenate([pool_ref[:, at], others_ref[:, at]], axis=0)
    qdir = jnp.dot(coef_ref[...], rows, preferred_element_type=F32)
    out_ref[...] = (qdir - wide(q_ref[:, at]) * column_ref[:, :1]).astype(BF16)


def far_kernel(n, *refs):
    at = 0
    for kept_ref, got_ref in zip(refs[:n], refs[n : 2 * n]):
        total = kept_ref[...] + wide(got_ref[...])
        columns = slice(at, at + total.shape[1])
        at += total.shape[1]
        part = refs[2 * n].shape[0]
        for k, ref in enumerate(refs[2 * n :]):
            ref[:, columns] = total[k * part : (k + 1) * part].astype(ref.dtype)


def passage_kernel(n, p_ref, total_ref, *refs):
    out_ref = refs[n]
    pdir = total_ref[...]
    for r in refs[:n]:
        pdir = pdir + wide(r[...])
    f = wide(p_ref[...])
    scale = lax.rsqrt(jnp.sum(f * f, axis=1, keepdims=True) + norm_eps)
    unit = f * scale
    inner = jnp.sum(unit * pdir, axis=1, keepdims=True)
    out_ref[...] = (scale * (pdir - unit * inner)).astype(BF16)


def make_local(loop, narrow):
    stages = stage_masks(loop)

    def body(queries, passages, pos_ids, neg_ids, neg_mask, neg_counts, d_loss):
        me = lax.axis_index("loop").astype(jnp.int32).reshape(1)
        block, width = passages.shape
        count, slots = neg_ids.shape
        half = loop * block // 2
        core = stages[-1][1]

        def cross(x, mask):
            return swap(x, "loop", loop, mask)

        first = [passages] + [cross(passages, m) for m in stages[0][1:]]
        pool = [jnp.concatenate(first[k : k + 2], axis=0) for k in (0, 2)]
        for _, m in stages[1:-2]:
            pool = [jnp.concatenate(pool + [cross(t, m) for t in pool], axis=0)]
        pool = pool + [cross(t, stages[-2][1]) for t in pool]
        n = len(pool)

        others = cross(queries, core)
        row = lambda x: x.reshape(1, count)
        weights, pack = call(
            functools.partial(weight_kernel, stages, block),
            [((half, count), F32), ((half + 8, count), F32)],
            (me, neg_ids.T, neg_mask.T, row(neg_counts), row(pos_ids), row(d_loss), queries),
            in_specs=[SMEM] + [HBM] * 6,
            limit=WIDE_LIMIT,
            flops=10000000,
            scratch_shapes=[pltpu.VMEM((slots, count), jnp.int32)] * 2
            + [pltpu.VMEM((1, count), jnp.int32)] * 2
            + [pltpu.VMEM((1, count), F32), pltpu.SemaphoreType.DMA((5,))],
        )
        pack = cross(pack, core)

        both = 2 * count
        raw, scale, qs = call(
            functools.partial(early_kernel, n // 2),
            [((half // 2, both), F32), ((half // 2, 128), F32), ((1, both), F32)],
            (*pool[: n // 2], queries, others),
            flops=2 * half * count * width,
        )
        rows, raw, scale, terms, chosen, sums = call(
            functools.partial(late_kernel, n, stages, block),
            [((half, width), BF16), ((half, both), F32), ((half, 128), F32)] + [((half, both), F32)] * 2 + [((8, both), F32)],
            (me, *pool, queries, others, raw, scale, qs, weights, pack, row(pos_ids)),
            in_specs=[SMEM] + [VMEM] * (n + 8),
            flops=2 * half * count * width,
        )
        lead = width // 16 * 11
        piece = (half // 2, lead)
        kept0, sent0, coef, sums = call(
            coef_kernel,
            [(piece, F32), (piece, BF16), ((half, both), F32), ((8, both), F32)],
            (queries, others, qs, terms, chosen, sums, cross(sums, core), row(d_loss), pack),
            flops=2 * half * count * width,
        )
        near = stages[-2][1]
        got0 = cross(sent0, near)
        kept1, sent1 = call(
            other_columns_kernel,
            [((half // 2, width - lead), F32), ((half // 2, width - lead), BF16)],
            (queries, others, coef),
            flops=2 * half * count * width,
        )
        qc, share, loss, inner = call(
            share_kernel,
            [((half, count), BF16), ((half + 8, count), F32)] + [((1, count), F32)] * 2,
            (raw, scale, coef, sums),
        )

        kept, got = [kept0, kept1], [got0, cross(sent1, near)]
        for _, m in stages[1:-2][::-1]:
            total = jnp.concatenate(kept, axis=1) + wide(jnp.concatenate(got, axis=1))
            part = total.shape[0] // 2
            kept, got = [total[:part]], [cross(total[part:].astype(BF16), m)]
        term = (block, width)
        total, *terms = call(
            functools.partial(far_kernel, len(kept)), [(term, F32)] + [(term, BF16)] * 3, (*kept, *got)
        )
        moved = [cross(terms[k - 1], stages[0][k]) for k in (3, 2, 1)]
        for t in moved:
            total = total + wide(t)
        moved = []
        for b in range(narrow.bit_length() - 1):
            if moved:
                total = total + wide(moved.pop())
            moved.append(swap(total.astype(BF16), "narrow", narrow, 1 << b))

        step = 512
        calls = 2
        steps = width // step // calls
        grad_queries = []
        operands = (rows, cross(rows, core), qc, cross(share, core), inner, qs, queries)
        for k in range(calls):
            grad_queries = call(
                functools.partial(query_kernel, k * steps),
                [(queries.shape, BF16)],
                (*operands, *grad_queries),
                grid=(steps,),
                in_specs=[VMEM] * 7 + [pl.BlockSpec(memory_space=pl.ANY)] * len(grad_queries),
                out_specs=(pl.BlockSpec((count, step), lambda i, k=k: (0, i + k * steps)),),
                input_output_aliases={7: 0} if grad_queries else {},
                scratch_shapes=[pltpu.VMEM((count, 2 * half), BF16), pltpu.VMEM((count, 128), F32)],
                flops=4 * half * count * width // calls,
                moved=3000000,
            )
        (grad_passages,) = call(
            functools.partial(passage_kernel, len(moved)), [(passages.shape, BF16)], (passages, total, *moved)
        )
        return loss.reshape(count), *grad_queries, grad_passages

    return body


def solution(mesh):
    both = ("loop", "narrow")
    return jax.shard_map(
        make_local(mesh.shape["loop"], mesh.shape["narrow"]),
        mesh=mesh,
        in_specs=(P(both, None), P("loop", None), P(both), P(both, None), P(both, None), P(both), P(both)),
        out_specs=(P(both), P(both, None), P("loop", None)),
        check_vma=False,
    )
```
